512 devices in a mesh: dp: 8 (over z), section: 4 (over x), patch: 16 (over y, core).
Axes of the slice: x: 4, y: 8, z: 8, core: 2. Of those that a mesh axis runs over, the one named last changes fastest.
Arguments:
- maps: bfloat16 [4, 8, 1536, 256], P(None, 'dp', 'patch'), may hold values from -6 to 6
- upstream: bfloat16 [4, 8, 1536, 256], P(None, 'dp', 'patch'), may hold values from -6 to 6
- weights: bfloat16 [4, 2304, 256], P('section'), may hold values from -0.125 to 0.125
- neighbours: int32 [9, 1536], P(None, 'patch'), may hold values from 0 to 1535, as said below
Outputs:
- input_grads: bfloat16 [4, 4, 8, 1536, 256], P('section', None, 'dp', 'patch')
- weight_grads: bfloat16 [4, 2304, 256], P('section')
The draws below stay inside these ranges and needn't reach their ends.
Inputs may be any that keep to these rules, and one draw needn't show every extreme that they name: neighbours[0, p] = p; every entry is (p + d) mod 1536 with -32 <= d <= 32, and both d = 32 and d = -32 occur in every draw.
All inputs are finite; a program needn't handle non-finite values.
Results may differ from the reference program's by a relative error of at most 0.0063.
Values may be sent and summed in bfloat16 or wider, within the bound.
No kernel may reach another device: no remote copies, remote signals or barrier semaphores. Data moves between devices by JAX's collectives and lax.ppermute only.
A program may use at most 64 MiB of HBM per device.

```python
import jax
import jax.numpy as jnp
from jax import lax

C = 256
TAPS = 9
HALO = 32
MICRO = 4
LEVELS = 4
BATCH = 8
NPIX = 1536
N_SECTION = 4


def draw_neighbours(key, part):
    pixels = jnp.arange(NPIX, dtype=jnp.int32)
    offsets = jax.random.randint(key, (TAPS, NPIX), -HALO, HALO + 1, dtype=jnp.int32)
    rows = jnp.arange(TAPS, dtype=jnp.int32)[:, None]
    marked = (pixels % 64 == 0)[None, :]
    offsets = jnp.where(rows == 0, 0, offsets)
    offsets = jnp.where(marked & (rows == TAPS - 1), -HALO, offsets)
    offsets = jnp.where(marked & (rows == TAPS - 2), HALO, offsets)
    return jnp.mod(pixels[None, :] + offsets, NPIX).astype(jnp.int32)


def steps_of(rng, dims, pieces, low, top_value):
    factor_of, own = 1.0, jax.random.fold_in(rng, 6)
    for position, blocks in pieces:
        draws = jnp.exp(jax.random.uniform(jax.random.fold_in(own, position), (blocks,), jnp.float32, low / len(pieces), top_value / len(pieces)))
        factor_of = factor_of * jnp.repeat(draws, dims[position] // blocks).reshape([-1 if axis == position else 1 for axis in range(len(dims))])
    return factor_of


def scatter_about(stream_key, shape, deviation, most, shards=(), kind=jnp.bfloat16):
    loudness = steps_of(stream_key, shape, shards, -0.22, 0.18) if shards else 1.0
    array = jax.random.normal(stream_key, shape, jnp.float32) * deviation * loudness
    return jnp.minimum(jnp.maximum(array, -most), most).astype(kind)


def setup_inputs(seed: int = 0) -> dict:
    streams_of = jax.random.split(jax.random.key(seed), 5)
    return {
        "maps": scatter_about(streams_of[0], (MICRO, BATCH, NPIX, C), 1.0, 6.0, ((1, 8), (2, 16))),
        "upstream": scatter_about(streams_of[1], (MICRO, BATCH, NPIX, C), 1.0, 6.0, ((1, 8), (2, 16))),
        "weights": scatter_about(streams_of[2], (LEVELS, TAPS * C, C), (TAPS * C) ** -0.5, 0.125, ((0, 4),)),
        "neighbours": draw_neighbours(jax.random.fold_in(streams_of[4], 71), 0),
    }


def reference(maps, upstream, weights, neighbours):
    index_rows = neighbours.T.reshape(-1).astype(jnp.int32)
    npix = maps.shape[2]
    chans = maps.shape[3]
    taps = neighbours.shape[0]
    flat_maps = maps.reshape((-1, npix, chans))
    flat_up = upstream.reshape((-1, npix, chans))

    def one_map(carry, item):
        start, top = item
        inputs = []
        squashes = []
        level_in = start
        for level in range(N_SECTION):
            gathered = level_in[index_rows].reshape((npix, taps * chans))
            act = jnp.dot(gathered, weights[level], preferred_element_type=jnp.float32)
            squash = jnp.tanh(act)
            inputs.append(level_in)
            squashes.append(squash)
            level_in = (level_in.astype(jnp.float32) + squash).astype(jnp.bfloat16)
        grad = top
        grads_out = []
        new_carry = []
        for level in range(N_SECTION - 1, -1, -1):
            squash = squashes[level]
            pre = (grad.astype(jnp.float32) * (1.0 - squash * squash)).astype(jnp.bfloat16)
            gathered = inputs[level][index_rows].reshape((npix, taps * chans))
            term = lax.dot_general(gathered, pre, (((0,), (0,)), ((), ())), preferred_element_type=jnp.float32)
            new_carry.append(carry[level] + term)
            w_taps = weights[level].reshape((taps, chans, chans)).astype(jnp.float32)
            parts = jnp.einsum("qo,kio->qki", pre.astype(jnp.float32), w_taps)
            spread = jax.ops.segment_sum(parts.reshape((npix * taps, chans)), index_rows, num_segments=npix)
            grad = (grad.astype(jnp.float32) + spread).astype(jnp.bfloat16)
            grads_out.append(grad)
        new_carry = new_carry[::-1]
        grads_out = grads_out[::-1]
        return tuple(new_carry), jnp.stack(grads_out, 0)

    init = tuple(jnp.zeros((taps * chans, chans), jnp.float32) for level in range(N_SECTION))
    sums, grads = lax.scan(one_map, init, (flat_maps, flat_up))
    grads = grads.reshape((maps.shape[0], maps.shape[1], N_SECTION, npix, chans))
    input_grads = jnp.transpose(grads, (2, 0, 1, 3, 4))
    weight_grads = jnp.stack(sums, 0).astype(jnp.bfloat16)
    return input_grads, weight_grads
```

```python
import functools

import jax
import jax.numpy as jnp
from jax import lax
from jax.experimental import pallas as pl
from jax.experimental.pallas import tpu as pltpu
from jax.sharding import Mesh
from jax.sharding import PartitionSpec as P

HALO = 32
TAPS = 9
C = 256
PIX = 96
LEVELS = 4
REACH = 2 * LEVELS * HALO
TILE = 64
PAD = 32
WIN = PIX + 2 * REACH
ROWS = WIN + 2 * PAD
HALF = TAPS * C // 2
BF = jnp.bfloat16
F32 = jnp.float32
NT = (((1,), (1,)), ((), ()))

FWD_TILES = ((0, 9), (1, 9), (1, 8), (2, 8))
PRE_ROWS = ((224, 384), (192, 416), (160, 448), (128, 480))
BWD_TILES = ((4, 6), (3, 6), (3, 7), (2, 7))
OWN = REACH
HROWS, PROWS, GROWS = PIX, PIX + HALO, PIX
MSG = HROWS + PROWS + GROWS


def stack_kernel(core_ref, m3a, m2a, m1a, own, m1b, m2b, m3b, w_mine, w_other, out_ref, offp_ref,
                 w_buf, h_buf, off_buf, s_buf, st_buf, gat, der, pre_buf, g_buf, sems):
    core = core_ref[0]
    copies = []
    for n, (src, half) in enumerate(((w_mine, core), (w_other, 1 - core))):
        row = pl.multiple_of(half * HALF, HALF)
        copies.append(pltpu.make_async_copy(src, w_buf.at[:, pl.ds(row, HALF), :], sems.at[n]))
        copies[-1].start()

    h_buf[...] = jnp.zeros_like(h_buf)
    off_buf[...] = jnp.zeros_like(off_buf)
    pre_buf[...] = jnp.zeros_like(pre_buf)
    g_buf[...] = jnp.zeros_like(g_buf)
    at = PAD
    for piece in (m3a, m2a, m1a, own, m1b, m2b, m3b):
        n = piece.shape[0]
        h_buf[0, at:at + n, :] = piece[:, :C]
        off_buf[at:at + n, :] = piece[:, C:C + 128].astype(F32)
        if piece.shape[1] > C + 128:
            g_buf[at:at + n, :] = piece[:, C + 128:]
        at += n

    rel = (lax.broadcasted_iota(jnp.int32, (TILE, 128), 1)
           - lax.broadcasted_iota(jnp.int32, (TILE, 128), 0) - HALO).astype(F32)

    def build_s(t, carry):
        d = off_buf[pl.ds(pl.multiple_of(t * TILE + PAD, PAD), TILE), :]
        for k in range(1, TAPS):
            hit = rel == d[:, k:k + 1]
            s_buf[t, (k - 1) * TILE:k * TILE, :] = jnp.where(hit, 1.0, 0.0).astype(BF)
        return carry

    lax.fori_loop(0, FWD_TILES[0][1], build_s, 0)

    def build_st(t, carry):
        d = jnp.transpose(off_buf[pl.ds(pl.multiple_of(t * TILE, TILE), 128), :])
        for k in range(1, TAPS):
            hit = -rel == d[k:k + 1, :]
            st_buf[t, (k - 1) * TILE:k * TILE, :] = jnp.where(hit, 1.0, 0.0).astype(BF)
        return carry

    lax.fori_loop(BWD_TILES[3][0], BWD_TILES[3][1], build_st, 0)

    for copy in copies:
        copy.wait()

    for level in range(LEVELS):
        first, last = FWD_TILES[level]

        def gather(t, carry, level=level):
            src = h_buf[level, pl.ds(pl.multiple_of(t * TILE, TILE), 2 * TILE), :]
            dst = pl.ds(pl.multiple_of(t * TILE, TILE), TILE)
            rows = jnp.dot(s_buf[t], src, preferred_element_type=F32).astype(BF)
            gat[dst, :C] = src[PAD:PAD + TILE]
            for k in range(1, TAPS):
                gat[dst, k * C:(k + 1) * C] = rows[(k - 1) * TILE:k * TILE]
            return carry

        lax.fori_loop(first, last, gather, 0)
        lo, hi = first * TILE, last * TILE
        act = jnp.dot(gat[lo:hi, :], w_buf[level], preferred_element_type=F32)
        squash = jnp.tanh(act)
        der[level, lo:hi, :] = 1.0 - squash * squash
        if level + 1 < LEVELS:
            h_buf[level + 1, PAD + lo:PAD + hi, :] = (
                h_buf[level, PAD + lo:PAD + hi, :].astype(F32) + squash).astype(BF)
        out_ref[level, :HROWS, :] = h_buf[level, PAD + OWN:PAD + OWN + PIX, :]

    for level in range(LEVELS - 1, -1, -1):
        lo, hi = PRE_ROWS[level]
        pre_buf[PAD + lo:PAD + hi, :] = (
            g_buf[PAD + lo:PAD + hi, :].astype(F32) * der[level, lo:hi, :]).astype(BF)
        first, last = BWD_TILES[level]

        def spread(t, carry):
            src = pre_buf[pl.ds(pl.multiple_of(t * TILE, TILE), 2 * TILE), :]
            dst = pl.ds(pl.multiple_of(t * TILE, TILE), TILE)
            rows = jnp.dot(st_buf[t], src, preferred_element_type=F32).astype(BF)
            gat[dst, :C] = src[PAD:PAD + TILE]
            for k in range(1, TAPS):
                gat[dst, k * C:(k + 1) * C] = rows[(k - 1) * TILE:k * TILE]
            return carry

        lax.fori_loop(first, last, spread, 0)
        lo, hi = first * TILE, last * TILE
        total = g_buf[PAD + lo:PAD + hi, :].astype(F32)
        for k in range(TAPS):
            total = total + lax.dot_general(gat[lo:hi, k * C:(k + 1) * C],
                                            w_buf[level, k * C:(k + 1) * C, :], NT,
                                            preferred_element_type=F32)
        g_buf[PAD + lo:PAD + hi, :] = total.astype(BF)
        start = pl.multiple_of(PAD + OWN - HALO + HALO * core, HALO)
        out_ref[level, HROWS:HROWS + PROWS, :] = pre_buf[pl.ds(start, PROWS), :]
        out_ref[level, HROWS + PROWS:, :] = g_buf[PAD + OWN:PAD + OWN + PIX, :]

    start = pl.multiple_of(PAD + OWN - HALO - PIX * core, HALO)
    offp_ref[...] = off_buf[pl.ds(start, 2 * PROWS), :]


def grad_kernel(core_ref, mine, other, offp, out_ref, gin_ref, st_buf, p_buf, h_buf, t_buf):
    core = core_ref[0]
    micro = mine.shape[0]
    pair = 2 * PIX
    gin_ref[...] = mine[:, HROWS + PROWS:, :]
    for c in range(2):
        @pl.when(core == c)
        def _(c=c):
            both = (mine, other) if c == 0 else (other, mine)
            for m in range(micro):
                for n, ref in enumerate(both):
                    p_buf[n * PROWS:(n + 1) * PROWS, m * 128:(m + 1) * 128] = (
                        ref[m, HROWS:HROWS + PROWS, c * 128:(c + 1) * 128])
                    h_buf[m * pair + n * PIX:m * pair + (n + 1) * PIX, :] = ref[m, :HROWS, :]
    rel = (lax.broadcasted_iota(jnp.int32, (pair, 2 * PROWS), 0)
           - lax.broadcasted_iota(jnp.int32, (pair, 2 * PROWS), 1) + HALO).astype(F32)
    offt = jnp.transpose(offp[...])
    h_t = jnp.transpose(h_buf[...].astype(F32)).astype(BF)
    pre = p_buf[...]
    for k in range(TAPS):
        if k == 0:
            spread = pre[HALO:HALO + pair]
        else:
            hit = jnp.where(rel == offt[k:k + 1, :], 1.0, 0.0).astype(BF)
            spread = jnp.dot(hit, pre, preferred_element_type=F32).astype(BF)
        for m in range(micro):
            t_buf[m * pair:(m + 1) * pair, :] = spread[:, m * 128:(m + 1) * 128]
        block = jnp.dot(h_t, t_buf[...], preferred_element_type=F32)
        out_ref[k * C:(k + 1) * C, :] = block.astype(BF)
    out_ref[TAPS * C:, :] = jnp.zeros((out_ref.shape[0] - TAPS * C, 128), BF)


def sum_kernel(x_ref, out_ref):
    total = jnp.sum(x_ref[...].astype(F32), axis=0).astype(BF)
    out_ref[...] = jnp.broadcast_to(total[None], out_ref.shape)


def join_kernel(core_ref, mine, other, out_ref):
    for c in range(2):
        @pl.when(core_ref[0] == c)
        def _(c=c):
            rows = out_ref.shape[0]
            out_ref[:, c * 128:(c + 1) * 128] = mine[:rows]
            out_ref[:, (1 - c) * 128:(2 - c) * 128] = other[:rows]


VMEM = pl.BlockSpec(memory_space=pltpu.VMEM)
SMEM = pl.BlockSpec(memory_space=pltpu.SMEM)
ANY = pl.BlockSpec(memory_space=pl.ANY)
INTERPRET = False


def call(kernel, out_shape, in_specs, scratch=(), flops=0, nbytes=0):
    many = isinstance(out_shape, (tuple, list))
    return pl.pallas_call(
        kernel,
        out_shape=out_shape,
        in_specs=in_specs,
        out_specs=[VMEM] * len(out_shape) if many else VMEM,
        scratch_shapes=list(scratch),
        interpret=INTERPRET,
        cost_estimate=pl.CostEstimate(flops=flops, bytes_accessed=nbytes, transcendentals=0),
        compiler_params=pltpu.CompilerParams(vmem_limit_bytes=48 << 20),
    )


def shift(axis_size, by):
    return [(i, (i + by) % axis_size) for i in range(axis_size)]


def body(maps, upstream, weights, neighbours):
    micro = maps.shape[0]
    section = lax.axis_index("section")
    core = lax.axis_index("core")
    patches = lax.axis_size("py") * lax.axis_size("core")
    patch = lax.axis_index("py") * lax.axis_size("core") + core
    npix = PIX * patches
    cores = core.reshape((1,)).astype(jnp.int32)

    half = lax.dynamic_slice_in_dim(weights[0], core * HALF, HALF, axis=0)
    w_mine = lax.all_gather(half, "section")
    w_other = lax.ppermute(w_mine, "core", shift(2, 1))

    place = patch * PIX + jnp.arange(PIX, dtype=jnp.int32)
    offsets = jnp.mod(neighbours - place[None, :] + HALO, npix) - HALO
    offsets = jnp.pad(offsets.astype(BF).T, ((0, 0), (0, 128 - TAPS)))
    start = lax.dynamic_index_in_dim(maps, section, 0, keepdims=False)[0]
    top = lax.dynamic_index_in_dim(upstream, section, 0, keepdims=False)[0]
    own = jnp.concatenate([start, offsets, top], axis=1)
    edge = 2 * HALO
    send = functools.partial(lax.ppermute, axis_name=("py", "core"))
    m1a = send(own, perm=shift(patches, 1))
    m1b = send(own, perm=shift(patches, -1))
    m2a = send(own, perm=shift(patches, 2))
    m2b = send(own, perm=shift(patches, -2))
    m3a = send(own[PIX - edge:, :C + 128], perm=shift(patches, 3))
    m3b = send(own[:edge, :C + 128], perm=shift(patches, -3))

    tiles = FWD_TILES[0][1]
    out, offp = call(
        stack_kernel,
        [jax.ShapeDtypeStruct((LEVELS, MSG, C), BF), jax.ShapeDtypeStruct((2 * PROWS, 128), F32)],
        [SMEM] + [VMEM] * 7 + [ANY] * 2,
        [
            pltpu.VMEM((LEVELS, TAPS * C, C), BF),
            pltpu.VMEM((LEVELS, ROWS, C), BF),
            pltpu.VMEM((ROWS, 128), F32),
            pltpu.VMEM((tiles, (TAPS - 1) * TILE, 2 * TILE), BF),
            pltpu.VMEM((BWD_TILES[3][1], (TAPS - 1) * TILE, 2 * TILE), BF),
            pltpu.VMEM((tiles * TILE, TAPS * C), BF),
            pltpu.VMEM((LEVELS, tiles * TILE, C), F32),
            pltpu.VMEM((ROWS, C), BF),
            pltpu.VMEM((ROWS, C), BF),
            pltpu.SemaphoreType.DMA((2,)),
        ],
        flops=6 * 10**9, nbytes=6 * 10**6,
    )(cores, m3a, m2a, m1a, own, m1b, m2b, m3b, w_mine, w_other)

    mine = lax.all_to_all(out, "section", 0, 0, tiled=True)
    other = lax.ppermute(mine[:, :HROWS + PROWS], "core", shift(2, 1))
    chips = lax.axis_size("dp") * lax.axis_size("py")
    rows = (TAPS + 1) * C
    part, gin = call(
        grad_kernel,
        [jax.ShapeDtypeStruct((rows, 128), BF), jax.ShapeDtypeStruct((micro, PIX, C), BF)],
        [SMEM] + [VMEM] * 3,
        [
            pltpu.VMEM((2 * PIX, 2 * PROWS), BF),
            pltpu.VMEM((2 * PROWS, micro * 128), BF),
            pltpu.VMEM((micro * 2 * PIX, C), BF),
            pltpu.VMEM((micro * 2 * PIX, 128), BF),
        ],
        flops=10**9, nbytes=2 * 10**6,
    )(cores, mine, other, offp)
    pieces = lax.all_to_all(part.reshape((chips, rows // chips, 128)), ("dp", "py"), 0, 0, tiled=True)
    total = call(
        sum_kernel, jax.ShapeDtypeStruct(pieces.shape, BF), [VMEM], nbytes=10**6,
    )(pieces)
    full = lax.all_to_all(total, ("dp", "py"), 0, 0, tiled=True).reshape((rows, 128))
    swapped = lax.ppermute(full, "core", shift(2, 1))
    summed = call(
        join_kernel, jax.ShapeDtypeStruct((TAPS * C, C), BF), [SMEM, VMEM, VMEM], nbytes=2 * 10**6,
    )(cores, full, swapped)
    return (gin[None, :, None], summed[None])


def solution(mesh):
    size = dict(mesh.shape)
    grid = (size["dp"], size["section"], size["patch"] // 2, 2)
    fine = Mesh(mesh.devices.reshape(grid), ("dp", "section", "py", "core"))
    patch = ("py", "core")
    in_specs = (
        P(None, "dp", patch, None),
        P(None, "dp", patch, None),
        P("section", None, None),
        P(None, patch),
    )
    out_specs = (P("section", None, "dp", patch, None), P("section", None, None))
    return jax.shard_map(body, mesh=fine, in_specs=in_specs, out_specs=out_specs, check_vma=False)
```

```python
import functools

import jax
import jax.numpy as jnp
from jax import lax
from jax.experimental import pallas as pl
from jax.experimental.pallas import tpu as pltpu
from jax.sharding import Mesh
from jax.sharding import PartitionSpec as P


HALO = 32
TAPS = 9
C = 256
PIX = 96
LEVELS = 4
REACH = 2 * LEVELS * HALO
TILE = 64
PAD = 32
WIN = PIX + 2 * REACH
ROWS = WIN + 2 * PAD
HALF = TAPS * C // 2
BF = jnp.bfloat16
F32 = jnp.float32
NT = (((1,), (1,)), ((), ()))

FWD_TILES = ((0, 9), (1, 9), (1, 8), (2, 8))
PRE_ROWS = ((224, 384), (192, 416), (160, 448), (128, 480))
BWD_TILES = ((4, 6), (3, 6), (3, 7), (2, 7))
OWN = REACH
HROWS, PROWS, GROWS = PIX, PIX + HALO, PIX
MSG = HROWS + PROWS + GROWS


def stack_kernel(ids_ref, m3a, m2a, m1a, own, m1b, m2b, m3b, w_own, *refs):
    parts, refs = refs[:8], refs[8:]
    out_ref, offp_ref, w_buf, h_buf, off_buf, s_buf, st_buf, gat, der, pre_buf, g_buf, sems = refs
    core, section = ids_ref[0], ids_ref[1]
    copies = [pltpu.make_async_copy(w_own, w_buf.at[section], sems.at[0])]
    for n, (hop, first) in enumerate(((3, 0), (1, 0), (2, 0), (2, HALF // 2))):
        for side in range(2):
            src = parts[2 * n + side]
            row = pl.multiple_of(jnp.abs(core - side) * HALF + first, HALF // 2)
            dst = w_buf.at[lax.rem(section + hop, LEVELS), pl.ds(row, src.shape[0]), :]
            copies.append(pltpu.make_async_copy(src, dst, sems.at[2 * n + side + 1]))
    for copy in copies:
        copy.start()

    h_buf[...] = jnp.zeros_like(h_buf)
    off_buf[...] = jnp.zeros_like(off_buf)
    pre_buf[...] = jnp.zeros_like(pre_buf)
    g_buf[...] = jnp.zeros_like(g_buf)
    at = PAD
    for piece in (m3a, m2a, m1a, own, m1b, m2b, m3b):
        n = piece.shape[0]
        h_buf[0, at:at + n, :] = piece[:, :C]
        off_buf[at:at + n, :] = piece[:, C:C + 128].astype(F32)
        if piece.shape[1] > C + 128:
            g_buf[at:at + n, :] = piece[:, C + 128:]
        at += n

    rel = (lax.broadcasted_iota(jnp.int32, (TILE, 128), 1)
           - lax.broadcasted_iota(jnp.int32, (TILE, 128), 0) - HALO).astype(F32)

    def build_s(t, carry):
        d = off_buf[pl.ds(pl.multiple_of(t * TILE + PAD, PAD), TILE), :]
        for k in range(1, TAPS):
            hit = rel == d[:, k:k + 1]
            s_buf[t, (k - 1) * TILE:k * TILE, :] = jnp.where(hit, 1.0, 0.0).astype(BF)
        return carry

    lax.fori_loop(0, FWD_TILES[0][1], build_s, 0)

    def build_st(t, carry):
        d = jnp.transpose(off_buf[pl.ds(pl.multiple_of(t * TILE, TILE), 128), :])
        for k in range(1, TAPS):
            hit = -rel == d[k:k + 1, :]
            st_buf[t, (k - 1) * TILE:k * TILE, :] = jnp.where(hit, 1.0, 0.0).astype(BF)
        return carry

    lax.fori_loop(BWD_TILES[3][0], BWD_TILES[3][1], build_st, 0)

    for copy in copies:
        copy.wait()

    for level in range(LEVELS):
        first, last = FWD_TILES[level]

        def gather(t, carry, level=level):
            src = h_buf[level, pl.ds(pl.multiple_of(t * TILE, TILE), 2 * TILE), :]
            dst = pl.ds(pl.multiple_of(t * TILE, TILE), TILE)
            rows = jnp.dot(s_buf[t], src, preferred_element_type=F32).astype(BF)
            gat[dst, :C] = src[PAD:PAD + TILE]
            for k in range(1, TAPS):
                gat[dst, k * C:(k + 1) * C] = rows[(k - 1) * TILE:k * TILE]
            return carry

        lax.fori_loop(first, last, gather, 0)
        lo, hi = first * TILE, last * TILE
        act = jnp.dot(gat[lo:hi, :], w_buf[level], preferred_element_type=F32)
        squash = jnp.tanh(act)
        der[level, lo:hi, :] = 1.0 - squash * squash
        if level + 1 < LEVELS:
            h_buf[level + 1, PAD + lo:PAD + hi, :] = (
                h_buf[level, PAD + lo:PAD + hi, :].astype(F32) + squash).astype(BF)
        out_ref[level, :HROWS, :] = h_buf[level, PAD + OWN:PAD + OWN + PIX, :]

    for level in range(LEVELS - 1, -1, -1):
        lo, hi = PRE_ROWS[level]
        pre_buf[PAD + lo:PAD + hi, :] = (
            g_buf[PAD + lo:PAD + hi, :].astype(F32) * der[level, lo:hi, :]).astype(BF)
        first, last = BWD_TILES[level]

        def spread(t, carry):
            src = pre_buf[pl.ds(pl.multiple_of(t * TILE, TILE), 2 * TILE), :]
            dst = pl.ds(pl.multiple_of(t * TILE, TILE), TILE)
            rows = jnp.dot(st_buf[t], src, preferred_element_type=F32).astype(BF)
            gat[dst, :C] = src[PAD:PAD + TILE]
            for k in range(1, TAPS):
                gat[dst, k * C:(k + 1) * C] = rows[(k - 1) * TILE:k * TILE]
            return carry

        lax.fori_loop(first, last, spread, 0)
        lo, hi = first * TILE, last * TILE
        total = g_buf[PAD + lo:PAD + hi, :].astype(F32)
        for k in range(TAPS):
            total = total + lax.dot_general(gat[lo:hi, k * C:(k + 1) * C],
                                            w_buf[level, k * C:(k + 1) * C, :], NT,
                                            preferred_element_type=F32)
        g_buf[PAD + lo:PAD + hi, :] = total.astype(BF)
        start = pl.multiple_of(PAD + OWN - HALO + HALO * core, HALO)
        out_ref[level, HROWS:HROWS + PROWS, :] = pre_buf[pl.ds(start, PROWS), :]
        out_ref[level, HROWS + PROWS:, :] = g_buf[PAD + OWN:PAD + OWN + PIX, :]

    start = pl.multiple_of(PAD + OWN - HALO - PIX * core, HALO)
    offp_ref[...] = off_buf[pl.ds(start, 2 * PROWS), :]


def grad_kernel(core_ref, mine, other, offp, out_ref, gin_ref, st_buf, p_buf, h_buf, t_buf):
    core = core_ref[0]
    micro = mine.shape[0]
    pair = 2 * PIX
    gin_ref[...] = mine[:, HROWS + PROWS:, :]
    for c in range(2):
        @pl.when(core == c)
        def _(c=c):
            both = (mine, other) if c == 0 else (other, mine)
            for m in range(micro):
                for n, ref in enumerate(both):
                    p_buf[n * PROWS:(n + 1) * PROWS, m * 128:(m + 1) * 128] = (
                        ref[m, HROWS:HROWS + PROWS, c * 128:(c + 1) * 128])
                    h_buf[m * pair + n * PIX:m * pair + (n + 1) * PIX, :] = ref[m, :HROWS, :]
    rel = (lax.broadcasted_iota(jnp.int32, (pair, 2 * PROWS), 0)
           - lax.broadcasted_iota(jnp.int32, (pair, 2 * PROWS), 1) + HALO).astype(F32)
    offt = jnp.transpose(offp[...])
    h_t = jnp.transpose(h_buf[...].astype(F32)).astype(BF)
    pre = p_buf[...]
    for k in range(TAPS):
        if k == 0:
            spread = pre[HALO:HALO + pair]
        else:
            hit = jnp.where(rel == offt[k:k + 1, :], 1.0, 0.0).astype(BF)
            spread = jnp.dot(hit, pre, preferred_element_type=F32).astype(BF)
        for m in range(micro):
            t_buf[m * pair:(m + 1) * pair, :] = spread[:, m * 128:(m + 1) * 128]
        block = jnp.dot(h_t, t_buf[...], preferred_element_type=F32)
        out_ref[k * C:(k + 1) * C, :] = block.astype(BF)
    out_ref[TAPS * C:, :] = jnp.zeros((out_ref.shape[0] - TAPS * C, 128), BF)


def sum_kernel(x_ref, out_ref):
    total = jnp.sum(x_ref[...].astype(F32), axis=0).astype(BF)
    out_ref[...] = jnp.broadcast_to(total[None], out_ref.shape)


def join_kernel(core_ref, mine, other, out_ref):
    for c in range(2):
        @pl.when(core_ref[0] == c)
        def _(c=c):
            rows = out_ref.shape[0]
            out_ref[:, c * 128:(c + 1) * 128] = mine[:rows]
            out_ref[:, (1 - c) * 128:(2 - c) * 128] = other[:rows]


VMEM = pl.BlockSpec(memory_space=pltpu.VMEM)
SMEM = pl.BlockSpec(memory_space=pltpu.SMEM)
ANY = pl.BlockSpec(memory_space=pl.ANY)
INTERPRET = False


def call(kernel, out_shape, in_specs, scratch=(), flops=0, nbytes=0):
    many = isinstance(out_shape, (tuple, list))
    return pl.pallas_call(
        kernel,
        out_shape=out_shape,
        in_specs=in_specs,
        out_specs=[VMEM] * len(out_shape) if many else VMEM,
        scratch_shapes=list(scratch),
        interpret=INTERPRET,
        cost_estimate=pl.CostEstimate(flops=flops, bytes_accessed=nbytes, transcendentals=0),
        compiler_params=pltpu.CompilerParams(vmem_limit_bytes=48 << 20),
    )


def shift(axis_size, by):
    return [(i, (i + by) % axis_size) for i in range(axis_size)]


def step(maps, upstream, weights, neighbours):
    micro = maps.shape[0]
    section = lax.axis_index("section")
    core = lax.axis_index("core")
    patches = lax.axis_size("py") * lax.axis_size("core")
    patch = lax.axis_index("py") * lax.axis_size("core") + core
    npix = PIX * patches
    cores = jnp.stack([core, section]).astype(jnp.int32)

    sections = lax.axis_size("section")
    half = lax.dynamic_slice_in_dim(weights[0], core * HALF, HALF, axis=0)
    left = lax.ppermute(half, "section", shift(sections, 1))
    right = lax.ppermute(half, "section", shift(sections, -1))
    far_top = lax.ppermute(left[:HALF // 2], "section", shift(sections, 1))
    far_bottom = lax.ppermute(right[HALF // 2:], "section", shift(sections, -1))
    parts = []
    for block in (left, right, far_top, far_bottom):
        parts += [block, lax.ppermute(block, "core", shift(2, 1))]

    place = patch * PIX + jnp.arange(PIX, dtype=jnp.int32)
    offsets = jnp.mod(neighbours - place[None, :] + HALO, npix) - HALO
    offsets = jnp.pad(offsets.astype(BF).T, ((0, 0), (0, 128 - TAPS)))
    start = lax.dynamic_index_in_dim(maps, section, 0, keepdims=False)[0]
    top = lax.dynamic_index_in_dim(upstream, section, 0, keepdims=False)[0]
    own = jnp.concatenate([start, offsets, top], axis=1)
    edge = 2 * HALO
    send = functools.partial(lax.ppermute, axis_name=("py", "core"))
    m1a = send(own, perm=shift(patches, 1))
    m1b = send(own, perm=shift(patches, -1))
    m2a = send(own, perm=shift(patches, 2))
    m2b = send(own, perm=shift(patches, -2))
    m3a = send(own[PIX - edge:, :C + 128], perm=shift(patches, 3))
    m3b = send(own[:edge, :C + 128], perm=shift(patches, -3))

    tiles = FWD_TILES[0][1]
    out, offp = call(
        stack_kernel,
        [jax.ShapeDtypeStruct((LEVELS, MSG, C), BF), jax.ShapeDtypeStruct((2 * PROWS, 128), F32)],
        [SMEM] + [VMEM] * 7 + [ANY] * 9,
        [
            pltpu.VMEM((LEVELS, TAPS * C, C), BF),
            pltpu.VMEM((LEVELS, ROWS, C), BF),
            pltpu.VMEM((ROWS, 128), F32),
            pltpu.VMEM((tiles, (TAPS - 1) * TILE, 2 * TILE), BF),
            pltpu.VMEM((BWD_TILES[3][1], (TAPS - 1) * TILE, 2 * TILE), BF),
            pltpu.VMEM((tiles * TILE, TAPS * C), BF),
            pltpu.VMEM((LEVELS, tiles * TILE, C), F32),
            pltpu.VMEM((ROWS, C), BF),
            pltpu.VMEM((ROWS, C), BF),
            pltpu.SemaphoreType.DMA((9,)),
        ],
        flops=6 * 10**9, nbytes=6 * 10**6,
    )(cores, m3a, m2a, m1a, own, m1b, m2b, m3b, weights[0], *parts)

    mine = lax.all_to_all(out, "section", 0, 0, tiled=True)
    other = lax.ppermute(mine[:, :HROWS + PROWS], "core", shift(2, 1))
    chips = lax.axis_size("dp") * lax.axis_size("py")
    rows = (TAPS + 1) * C
    part, gin = call(
        grad_kernel,
        [jax.ShapeDtypeStruct((rows, 128), BF), jax.ShapeDtypeStruct((micro, PIX, C), BF)],
        [SMEM] + [VMEM] * 3,
        [
            pltpu.VMEM((2 * PIX, 2 * PROWS), BF),
            pltpu.VMEM((2 * PROWS, micro * 128), BF),
            pltpu.VMEM((micro * 2 * PIX, C), BF),
            pltpu.VMEM((micro * 2 * PIX, 128), BF),
        ],
        flops=10**9, nbytes=2 * 10**6,
    )(cores, mine, other, offp)
    pieces = lax.all_to_all(part.reshape((chips, rows // chips, 128)), ("dp", "py"), 0, 0, tiled=True)
    total = call(
        sum_kernel, jax.ShapeDtypeStruct(pieces.shape, BF), [VMEM], nbytes=10**6,
    )(pieces)
    full = lax.all_to_all(total, ("dp", "py"), 0, 0, tiled=True).reshape((rows, 128))
    swapped = lax.ppermute(full, "core", shift(2, 1))
    summed = call(
        join_kernel, jax.ShapeDtypeStruct((TAPS * C, C), BF), [SMEM, VMEM, VMEM], nbytes=2 * 10**6,
    )(cores, full, swapped)
    return (gin[None, :, None], summed[None])


def solution(mesh):
    size = dict(mesh.shape)
    grid = (size["dp"], size["section"], size["patch"] // 2, 2)
    fine = Mesh(mesh.devices.reshape(grid), ("dp", "section", "py", "core"))
    patch = ("py", "core")
    in_specs = (
        P(None, "dp", patch, None),
        P(None, "dp", patch, None),
        P("section", None, None),
        P(None, patch),
    )
    out_specs = (P("section", None, "dp", patch, None), P("section", None, None))
    return jax.shard_map(step, mesh=fine, in_specs=in_specs, out_specs=out_specs, check_vma=False)
```

```python
import functools

import jax
import jax.numpy as jnp
from jax import lax
from jax.experimental import pallas as pl
from jax.experimental.pallas import tpu as pltpu
from jax.sharding import Mesh
from jax.sharding import PartitionSpec as P


HALO = 32
TAPS = 9
C = 256
PIX = 96
LEVELS = 4
REACH = 2 * LEVELS * HALO
TILE = 64
PAD = 32
WIN = PIX + 2 * REACH
ROWS = WIN + 2 * PAD
HALF = TAPS * C // 2
BF = jnp.bfloat16
F32 = jnp.float32
NT = (((1,), (1,)), ((), ()))

FWD_TILES = ((0, 9), (1, 9), (1, 8), (2, 8))
PRE_ROWS = ((224, 384), (192, 416), (160, 448), (128, 480))
BWD_TILES = ((4, 6), (3, 6), (3, 7), (2, 7))
OWN = REACH
HROWS, PROWS, GROWS = PIX, PIX + HALO, PIX
MSG = HROWS + PROWS + GROWS


def expand(gat, t, src, hot):
    rows = jnp.dot(hot, src, preferred_element_type=F32).astype(BF)
    dst = pl.ds(pl.multiple_of(t * TILE, TILE), TILE)
    gat[dst, :C] = src[PAD:PAD + TILE]
    for k in range(1, TAPS):
        gat[dst, k * C:(k + 1) * C] = rows[(k - 1) * TILE:k * TILE]


def expand_all(gat, first, last, src_ref, hot_ref, group):
    def one(t):
        expand(gat, t, src_ref[pl.ds(pl.multiple_of(t * TILE, TILE), 2 * TILE), :], hot_ref[t])

    def some(i, carry):
        for j in range(group):
            one(first + i * group + j)
        return carry

    whole = (last - first) // group
    if whole:
        lax.fori_loop(0, whole, some, 0)
    for t in range(first + whole * group, last):
        one(t)


def stack_kernel(ids_ref, m3a, m2a, m1a, own, m1b, m2b, m3b, w_own, near_mine, near_other, far_mine, far_other,
                 out_ref, offp_ref, w_buf, h_buf, off_buf, s_buf, st_buf, gat, der, pre_buf, g_buf, sems):
    core, section = ids_ref[0], ids_ref[1]
    left, right = lax.rem(section + 3, LEVELS), lax.rem(section + 1, LEVELS)
    far = w_buf.at[lax.rem(section + 2, LEVELS)]
    row_mine = pl.multiple_of(core * HALF, HALF)
    row_other = pl.multiple_of((1 - core) * HALF, HALF)
    copies = []
    for n, (src, dst) in enumerate((
        (w_own, w_buf.at[section]),
        (near_mine, w_buf.at[jnp.where(core == 0, left, right)]),
        (near_other, w_buf.at[jnp.where(core == 0, right, left)]),
        (far_mine, far.at[pl.ds(row_mine, HALF), :]),
        (far_other, far.at[pl.ds(row_other, HALF), :]),
    )):
        copies.append(pltpu.make_async_copy(src, dst, sems.at[n]))
        copies[-1].start()

    h_buf[...] = jnp.zeros_like(h_buf)
    off_buf[...] = jnp.zeros_like(off_buf)
    pre_buf[...] = jnp.zeros_like(pre_buf)
    g_buf[...] = jnp.zeros_like(g_buf)
    at = PAD
    for piece in (m3a, m2a, m1a, own, m1b, m2b, m3b):
        n = piece.shape[0]
        h_buf[0, at:at + n, :] = piece[:, :C]
        off_buf[at:at + n, :] = piece[:, C:C + 128].astype(F32)
        if piece.shape[1] > C + 128:
            g_buf[at:at + n, :] = piece[:, C + 128:]
        at += n

    rel = (lax.broadcasted_iota(jnp.int32, (TILE, 128), 1)
           - lax.broadcasted_iota(jnp.int32, (TILE, 128), 0) - HALO).astype(F32)

    def build_s(t, carry):
        d = off_buf[pl.ds(pl.multiple_of(t * TILE + PAD, PAD), TILE), :]
        for k in range(1, TAPS):
            hit = rel == d[:, k:k + 1]
            s_buf[t, (k - 1) * TILE:k * TILE, :] = jnp.where(hit, 1.0, 0.0).astype(BF)
        return carry

    lax.fori_loop(0, FWD_TILES[0][1], build_s, 0)

    def build_st(t, carry):
        d = jnp.transpose(off_buf[pl.ds(pl.multiple_of(t * TILE, TILE), 128), :])
        for k in range(1, TAPS):
            hit = -rel == d[k:k + 1, :]
            st_buf[t, (k - 1) * TILE:k * TILE, :] = jnp.where(hit, 1.0, 0.0).astype(BF)
        return carry

    lax.fori_loop(BWD_TILES[3][0], BWD_TILES[3][1], build_st, 0)

    for copy in copies:
        copy.wait()

    for level in range(LEVELS):
        first, last = FWD_TILES[level]

        expand_all(gat, first, last, h_buf.at[level], s_buf, 3)
        lo, hi = first * TILE, last * TILE
        act = jnp.dot(gat[lo:hi, :], w_buf[level], preferred_element_type=F32)
        squash = jnp.tanh(act)
        der[level, lo:hi, :] = 1.0 - squash * squash
        if level + 1 < LEVELS:
            h_buf[level + 1, PAD + lo:PAD + hi, :] = (
                h_buf[level, PAD + lo:PAD + hi, :].astype(F32) + squash).astype(BF)
        out_ref[level, :HROWS, :] = h_buf[level, PAD + OWN:PAD + OWN + PIX, :]

    for level in range(LEVELS - 1, -1, -1):
        lo, hi = PRE_ROWS[level]
        pre_buf[PAD + lo:PAD + hi, :] = (
            g_buf[PAD + lo:PAD + hi, :].astype(F32) * der[level, lo:hi, :]).astype(BF)
        first, last = BWD_TILES[level]

        expand_all(gat, first, last, pre_buf, st_buf, 3)
        lo, hi = first * TILE, last * TILE
        total = g_buf[PAD + lo:PAD + hi, :].astype(F32)
        for k in range(TAPS):
            total = total + lax.dot_general(gat[lo:hi, k * C:(k + 1) * C],
                                            w_buf[level, k * C:(k + 1) * C, :], NT,
                                            preferred_element_type=F32)
        g_buf[PAD + lo:PAD + hi, :] = total.astype(BF)
        start = pl.multiple_of(PAD + OWN - HALO + HALO * core, HALO)
        out_ref[level, HROWS:HROWS + PROWS, :] = pre_buf[pl.ds(start, PROWS), :]
        out_ref[level, HROWS + PROWS:, :] = g_buf[PAD + OWN:PAD + OWN + PIX, :]

    start = pl.multiple_of(PAD + OWN - HALO - PIX * core, HALO)
    offp_ref[...] = off_buf[pl.ds(start, 2 * PROWS), :]


def grad_kernel(core_ref, mine, other, offp, out_ref, gin_ref, st_buf, p_buf, h_buf, t_buf):
    core = core_ref[0]
    micro = mine.shape[0]
    pair = 2 * PIX
    gin_ref[...] = mine[:, HROWS + PROWS:, :]
    for c in range(2):
        @pl.when(core == c)
        def _(c=c):
            both = (mine, other) if c == 0 else (other, mine)
            for m in range(micro):
                for n, ref in enumerate(both):
                    p_buf[n * PROWS:(n + 1) * PROWS, m * 128:(m + 1) * 128] = (
                        ref[m, HROWS:HROWS + PROWS, c * 128:(c + 1) * 128])
                    h_buf[m * pair + n * PIX:m * pair + (n + 1) * PIX, :] = ref[m, :HROWS, :]
    rel = (lax.broadcasted_iota(jnp.int32, (pair, 2 * PROWS), 0)
           - lax.broadcasted_iota(jnp.int32, (pair, 2 * PROWS), 1) + HALO).astype(F32)
    offt = jnp.transpose(offp[...])
    h_t = jnp.transpose(h_buf[...].astype(F32)).astype(BF)
    pre = p_buf[...]
    for k in range(TAPS):
        if k == 0:
            spread = pre[HALO:HALO + pair]
        else:
            hit = jnp.where(rel == offt[k:k + 1, :], 1.0, 0.0).astype(BF)
            spread = jnp.dot(hit, pre, preferred_element_type=F32).astype(BF)
        for m in range(micro):
            t_buf[m * pair:(m + 1) * pair, :] = spread[:, m * 128:(m + 1) * 128]
        block = jnp.dot(h_t, t_buf[...], preferred_element_type=F32)
        out_ref[k * C:(k + 1) * C, :] = block.astype(BF)
    out_ref[TAPS * C:, :] = jnp.zeros((out_ref.shape[0] - TAPS * C, 128), BF)


def sum_kernel(x_ref, out_ref):
    total = jnp.sum(x_ref[...].astype(F32), axis=0).astype(BF)
    out_ref[...] = jnp.broadcast_to(total[None], out_ref.shape)


def join_kernel(core_ref, mine, other, out_ref):
    for c in range(2):
        @pl.when(core_ref[0] == c)
        def _(c=c):
            rows = out_ref.shape[0]
            out_ref[:, c * 128:(c + 1) * 128] = mine[:rows]
            out_ref[:, (1 - c) * 128:(2 - c) * 128] = other[:rows]


VMEM = pl.BlockSpec(memory_space=pltpu.VMEM)
SMEM = pl.BlockSpec(memory_space=pltpu.SMEM)
HBM = pl.BlockSpec(memory_space=pltpu.HBM)
INTERPRET = False


def call(kernel, out_shape, in_specs, scratch=(), flops=0, nbytes=0):
    many = isinstance(out_shape, (tuple, list))
    return pl.pallas_call(
        kernel,
        out_shape=out_shape,
        in_specs=in_specs,
        out_specs=[VMEM] * len(out_shape) if many else VMEM,
        scratch_shapes=list(scratch),
        interpret=INTERPRET,
        cost_estimate=pl.CostEstimate(flops=flops, bytes_accessed=nbytes, transcendentals=0),
        compiler_params=pltpu.CompilerParams(vmem_limit_bytes=48 << 20),
    )


def stack_call(*operands):
    tiles = FWD_TILES[0][1]
    return call(
        stack_kernel,
        [jax.ShapeDtypeStruct((LEVELS, MSG, C), BF), jax.ShapeDtypeStruct((2 * PROWS, 128), F32)],
        [SMEM] + [VMEM] * 7 + [HBM] * 5,
        [
            pltpu.VMEM((LEVELS, TAPS * C, C), BF),
            pltpu.VMEM((LEVELS, ROWS, C), BF),
            pltpu.VMEM((ROWS, 128), F32),
            pltpu.VMEM((tiles, (TAPS - 1) * TILE, 2 * TILE), BF),
            pltpu.VMEM((BWD_TILES[3][1], (TAPS - 1) * TILE, 2 * TILE), BF),
            pltpu.VMEM((tiles * TILE, TAPS * C), BF),
            pltpu.VMEM((LEVELS, tiles * TILE, C), F32),
            pltpu.VMEM((ROWS, C), BF),
            pltpu.VMEM((ROWS, C), BF),
            pltpu.SemaphoreType.DMA((5,)),
        ],
        flops=6 * 10**9, nbytes=6 * 10**6,
    )(*operands)


def shift(axis_size, by):
    return [(i, (i + by) % axis_size) for i in range(axis_size)]


def step(maps, upstream, weights, neighbours):
    micro = maps.shape[0]
    section = lax.axis_index("section")
    core = lax.axis_index("core")
    patches = lax.axis_size("py") * lax.axis_size("core")
    patch = lax.axis_index("py") * lax.axis_size("core") + core
    npix = PIX * patches
    cores = jnp.stack([core, section]).astype(jnp.int32)

    sections = lax.axis_size("section")
    ways = [(2 * i + c, 2 * ((i + (1, -1)[c]) % sections) + c) for i in range(sections) for c in range(2)]
    near = lax.ppermute(weights[0], ("section", "core"), ways)
    half = lax.dynamic_slice_in_dim(near, core * HALF, HALF, axis=0)
    far = lax.ppermute(half, ("section", "core"), ways)
    near_other = lax.ppermute(near, "core", shift(2, 1))
    far_other = lax.ppermute(far, "core", shift(2, 1))

    place = patch * PIX + jnp.arange(PIX, dtype=jnp.int32)
    offsets = jnp.mod(neighbours - place[None, :] + HALO, npix) - HALO
    offsets = jnp.pad(offsets.astype(BF).T, ((0, 0), (0, 128 - TAPS)))
    start = lax.dynamic_index_in_dim(maps, section, 0, keepdims=False)[0]
    top = lax.dynamic_index_in_dim(upstream, section, 0, keepdims=False)[0]
    own = jnp.concatenate([start, offsets, top], axis=1)
    edge = 2 * HALO
    send = functools.partial(lax.ppermute, axis_name=("py", "core"))
    m1a = send(own, perm=shift(patches, 1))
    m1b = send(own, perm=shift(patches, -1))
    m2a = send(own, perm=shift(patches, 2))
    m2b = send(own, perm=shift(patches, -2))
    m3a = send(own[PIX - edge:, :C + 128], perm=shift(patches, 3))
    m3b = send(own[:edge, :C + 128], perm=shift(patches, -3))

    out, offp = stack_call(cores, m3a, m2a, m1a, own, m1b, m2b, m3b, weights[0], near, near_other, far, far_other)

    mine = lax.all_to_all(out, "section", 0, 0, tiled=True)
    other = lax.ppermute(mine[:, :HROWS + PROWS], "core", shift(2, 1))
    chips = lax.axis_size("dp") * lax.axis_size("py")
    rows = (TAPS + 1) * C
    part, gin = call(
        grad_kernel,
        [jax.ShapeDtypeStruct((rows, 128), BF), jax.ShapeDtypeStruct((micro, PIX, C), BF)],
        [SMEM] + [VMEM] * 3,
        [
            pltpu.VMEM((2 * PIX, 2 * PROWS), BF),
            pltpu.VMEM((2 * PROWS, micro * 128), BF),
            pltpu.VMEM((micro * 2 * PIX, C), BF),
            pltpu.VMEM((micro * 2 * PIX, 128), BF),
        ],
        flops=10**9, nbytes=2 * 10**6,
    )(cores, mine, other, offp)
    pieces = lax.all_to_all(part.reshape((chips, rows // chips, 128)), ("dp", "py"), 0, 0, tiled=True)
    total = call(
        sum_kernel, jax.ShapeDtypeStruct(pieces.shape, BF), [VMEM], nbytes=10**6,
    )(pieces)
    full = lax.all_to_all(total, ("dp", "py"), 0, 0, tiled=True).reshape((rows, 128))
    swapped = lax.ppermute(full, "core", shift(2, 1))
    summed = call(
        join_kernel, jax.ShapeDtypeStruct((TAPS * C, C), BF), [SMEM, VMEM, VMEM], nbytes=2 * 10**6,
    )(cores, full, swapped)
    return (gin[None, :, None], summed[None])


def solution(mesh):
    size = dict(mesh.shape)
    grid = (size["dp"], size["section"], size["patch"] // 2, 2)
    fine = Mesh(mesh.devices.reshape(grid), ("dp", "section", "py", "core"))
    patch = ("py", "core")
    in_specs = (
        P(None, "dp", patch, None),
        P(None, "dp", patch, None),
        P("section", None, None),
        P(None, patch),
    )
    out_specs = (P("section", None, "dp", patch, None), P("section", None, None))
    return jax.shard_map(step, mesh=fine, in_specs=in_specs, out_specs=out_specs, check_vma=False)
```

```python
import functools

import jax
import jax.numpy as jnp
from jax import lax
from jax.experimental import pallas as pl
from jax.experimental.pallas import tpu as pltpu
from jax.sharding import Mesh
from jax.sharding import PartitionSpec as P


HALO = 32
TAPS = 9
C = 256
PIX = 96
LEVELS = 4
REACH = 2 * LEVELS * HALO
TILE = 64
PAD = 32
WIN = PIX + 2 * REACH
ROWS = WIN + 2 * PAD
HALF = TAPS * C // 2
BF = jnp.bfloat16
F32 = jnp.float32
NT = (((1,), (1,)), ((), ()))

FWD_TILES = ((0, 9), (1, 9), (1, 8), (2, 8))
PRE_ROWS = ((224, 384), (192, 416), (160, 448), (128, 480))
BWD_TILES = ((4, 6), (3, 6), (3, 7), (2, 7))
OWN = REACH
HROWS, PROWS, GROWS = PIX, PIX + HALO, PIX
MSG = HROWS + PROWS + GROWS


def expand(gat, t, src, hot):
    rows = jnp.dot(hot, src, preferred_element_type=F32).astype(BF)
    dst = pl.ds(pl.multiple_of(t * TILE, TILE), TILE)
    gat[dst, :C] = src[PAD:PAD + TILE]
    for k in range(1, TAPS):
        gat[dst, k * C:(k + 1) * C] = rows[(k - 1) * TILE:k * TILE]


def expand_all(gat, first, last, src_ref, hot_ref, group):
    def one(t):
        expand(gat, t, src_ref[pl.ds(pl.multiple_of(t * TILE, TILE), 2 * TILE), :], hot_ref[t])

    def some(i, carry):
        for j in range(group):
            one(first + i * group + j)
        return carry

    whole = (last - first) // group
    if whole:
        lax.fori_loop(0, whole, some, 0)
    for t in range(first + whole * group, last):
        one(t)


def prep_kernel(ids_ref, m3a, m2a, m1a, own, m1b, m2b, m3b, h_ref, g_ref, s_ref, st_ref, gat_ref, pair_ref, off_buf):
    core = ids_ref[0]
    h_ref[:PAD, :] = jnp.zeros((PAD, C), BF)
    h_ref[ROWS - PAD:, :] = jnp.zeros((PAD, C), BF)
    g_ref[...] = jnp.zeros_like(g_ref)
    off_buf[:PAD, :] = jnp.zeros((PAD, 128), F32)
    off_buf[ROWS - PAD:, :] = jnp.zeros((PAD, 128), F32)
    at = PAD
    for piece in (m3a, m2a, m1a, own, m1b, m2b, m3b):
        n = piece.shape[0]
        h_ref[at:at + n, :] = piece[:, :C]
        off_buf[at:at + n, :] = piece[:, C:C + 128].astype(F32)
        if piece.shape[1] > C + 128:
            g_ref[at:at + n, :] = piece[:, C + 128:]
        at += n

    rel = (lax.broadcasted_iota(jnp.int32, (TILE, 128), 1)
           - lax.broadcasted_iota(jnp.int32, (TILE, 128), 0) - HALO).astype(F32)

    def build_s(t, carry):
        d = off_buf[pl.ds(pl.multiple_of(t * TILE + PAD, PAD), TILE), :]
        for k in range(1, TAPS):
            hit = rel == d[:, k:k + 1]
            s_ref[t, (k - 1) * TILE:k * TILE, :] = jnp.where(hit, 1.0, 0.0).astype(BF)
        return carry

    lax.fori_loop(0, FWD_TILES[0][1], build_s, 0)

    def build_st(t, carry):
        d = jnp.transpose(off_buf[pl.ds(pl.multiple_of(t * TILE, TILE), 128), :])
        for k in range(1, TAPS):
            hit = -rel == d[k:k + 1, :]
            st_ref[t, (k - 1) * TILE:k * TILE, :] = jnp.where(hit, 1.0, 0.0).astype(BF)
        return carry

    lax.fori_loop(BWD_TILES[3][0], BWD_TILES[3][1], build_st, 0)
    expand_all(gat_ref, *FWD_TILES[0], h_ref, s_ref, 3)

    start = pl.multiple_of(PAD + OWN - HALO - PIX * core, HALO)
    offt = jnp.transpose(off_buf[pl.ds(start, 2 * PROWS), :])
    apart = (lax.broadcasted_iota(jnp.int32, (2 * PIX, 2 * PROWS), 0)
             - lax.broadcasted_iota(jnp.int32, (2 * PIX, 2 * PROWS), 1) + HALO).astype(F32)
    for k in range(1, TAPS):
        pair_ref[k - 1] = jnp.where(apart == offt[k:k + 1, :], 1.0, 0.0).astype(BF)


def stack_kernel(ids_ref, h0, g_top, s_buf, st_buf, gat0, w_own, near1_mine, near1_other, near2_mine, near2_other,
                 far_mine, far_other, out_ref, w_buf, h_buf, gat, der, pre_buf, g_buf, sems):
    core, section = ids_ref[0], ids_ref[1]
    left, right = lax.rem(section + 3, LEVELS), lax.rem(section + 1, LEVELS)
    mine = w_buf.at[jnp.where(core == 0, left, right)]
    other = w_buf.at[jnp.where(core == 0, right, left)]
    far = w_buf.at[lax.rem(section + 2, LEVELS)]
    here = pl.ds(pl.multiple_of(core * HALF, HALF), HALF)
    there = pl.ds(pl.multiple_of((1 - core) * HALF, HALF), HALF)
    copies = []
    for n, (src, dst) in enumerate((
        (w_own, w_buf.at[section]),
        (near1_mine, mine.at[here, :]),
        (near1_other, other.at[there, :]),
        (near2_mine, mine.at[there, :]),
        (near2_other, other.at[here, :]),
        (far_mine, far.at[here, :]),
        (far_other, far.at[there, :]),
    )):
        copies.append(pltpu.make_async_copy(src, dst, sems.at[n]))
        copies[-1].start()
    h_buf[...] = jnp.zeros_like(h_buf)
    pre_buf[...] = jnp.zeros_like(pre_buf)
    g_buf[...] = g_top[...]
    for copy in copies:
        copy.wait()

    for level in range(LEVELS):
        first, last = FWD_TILES[level]

        src = h0 if level == 0 else h_buf.at[level - 1]
        rows = gat0 if level == 0 else gat
        if level:
            expand_all(gat, first, last, src, s_buf, 3)
        lo, hi = first * TILE, last * TILE
        act = jnp.dot(rows[lo:hi, :], w_buf[level], preferred_element_type=F32)
        squash = jnp.tanh(act)
        der[level, lo:hi, :] = 1.0 - squash * squash
        if level + 1 < LEVELS:
            h_buf[level, PAD + lo:PAD + hi, :] = (src[PAD + lo:PAD + hi, :].astype(F32) + squash).astype(BF)
        out_ref[level, :HROWS, :] = src[PAD + OWN:PAD + OWN + PIX, :]

    for level in range(LEVELS - 1, -1, -1):
        lo, hi = PRE_ROWS[level]
        pre_buf[PAD + lo:PAD + hi, :] = (
            g_buf[PAD + lo:PAD + hi, :].astype(F32) * der[level, lo:hi, :]).astype(BF)
        first, last = BWD_TILES[level]

        expand_all(gat, first, last, pre_buf, st_buf, 3)
        lo, hi = first * TILE, last * TILE
        total = g_buf[PAD + lo:PAD + hi, :].astype(F32)
        for k in range(TAPS):
            total = total + lax.dot_general(gat[lo:hi, k * C:(k + 1) * C],
                                            w_buf[level, k * C:(k + 1) * C, :], NT,
                                            preferred_element_type=F32)
        g_buf[PAD + lo:PAD + hi, :] = total.astype(BF)
        start = pl.multiple_of(PAD + OWN - HALO + HALO * core, HALO)
        out_ref[level, HROWS:HROWS + PROWS, :] = pre_buf[pl.ds(start, PROWS), :]
        out_ref[level, HROWS + PROWS:, :] = g_buf[PAD + OWN:PAD + OWN + PIX, :]


def grad_kernel(core_ref, mine, other, hot, out_ref, gin_ref, p_buf, h_buf, t_buf):
    core = core_ref[0]
    micro = mine.shape[0]
    pair = 2 * PIX
    gin_ref[...] = mine[:, HROWS + PROWS:, :]
    for c in range(2):
        @pl.when(core == c)
        def _(c=c):
            both = (mine, other) if c == 0 else (other, mine)
            for m in range(micro):
                for n, ref in enumerate(both):
                    p_buf[n * PROWS:(n + 1) * PROWS, m * 128:(m + 1) * 128] = (
                        ref[m, HROWS:HROWS + PROWS, c * 128:(c + 1) * 128])
                    h_buf[m * pair + n * PIX:m * pair + (n + 1) * PIX, :] = ref[m, :HROWS, :]
    h_t = jnp.transpose(h_buf[...].astype(F32)).astype(BF)
    pre = p_buf[...]
    for k in range(TAPS):
        if k == 0:
            spread = pre[HALO:HALO + pair]
        else:
            spread = jnp.dot(hot[k - 1], pre, preferred_element_type=F32).astype(BF)
        for m in range(micro):
            t_buf[m * pair:(m + 1) * pair, :] = spread[:, m * 128:(m + 1) * 128]
        block = jnp.dot(h_t, t_buf[...], preferred_element_type=F32)
        out_ref[k * C:(k + 1) * C, :] = block.astype(BF)
    out_ref[TAPS * C:, :] = jnp.zeros((out_ref.shape[0] - TAPS * C, 128), BF)


def sum_kernel(x_ref, out_ref):
    total = jnp.sum(x_ref[...].astype(F32), axis=0).astype(BF)
    out_ref[...] = jnp.broadcast_to(total[None], out_ref.shape)


def join_kernel(core_ref, mine, other, out_ref):
    for c in range(2):
        @pl.when(core_ref[0] == c)
        def _(c=c):
            rows = out_ref.shape[0]
            out_ref[:, c * 128:(c + 1) * 128] = mine[:rows]
            out_ref[:, (1 - c) * 128:(2 - c) * 128] = other[:rows]


VMEM = pl.BlockSpec(memory_space=pltpu.VMEM)
SMEM = pl.BlockSpec(memory_space=pltpu.SMEM)
ANY = pl.BlockSpec(memory_space=pl.ANY)
INTERPRET = False


def call(kernel, out_shape, in_specs, scratch=(), flops=0, nbytes=0):
    many = isinstance(out_shape, (tuple, list))
    return pl.pallas_call(
        kernel,
        out_shape=out_shape,
        in_specs=in_specs,
        out_specs=[VMEM] * len(out_shape) if many else VMEM,
        scratch_shapes=list(scratch),
        interpret=INTERPRET,
        cost_estimate=pl.CostEstimate(flops=flops, bytes_accessed=nbytes, transcendentals=0),
        compiler_params=pltpu.CompilerParams(vmem_limit_bytes=48 << 20),
    )


def prep_call(*operands):
    tiles, hot = FWD_TILES[0][1], (TAPS - 1) * TILE
    return call(
        prep_kernel,
        [
            jax.ShapeDtypeStruct((ROWS, C), BF),
            jax.ShapeDtypeStruct((ROWS, C), BF),
            jax.ShapeDtypeStruct((tiles, hot, 2 * TILE), BF),
            jax.ShapeDtypeStruct((BWD_TILES[3][1], hot, 2 * TILE), BF),
            jax.ShapeDtypeStruct((tiles * TILE, TAPS * C), BF),
            jax.ShapeDtypeStruct((TAPS - 1, 2 * PIX, 2 * PROWS), BF),
        ],
        [SMEM] + [VMEM] * 7,
        [pltpu.VMEM((ROWS, 128), F32)],
        flops=10**9, nbytes=6 * 10**6,
    )(*operands)


def stack_call(*operands):
    tiles = FWD_TILES[0][1]
    return call(
        stack_kernel,
        jax.ShapeDtypeStruct((LEVELS, MSG, C), BF),
        [SMEM] + [VMEM] * 5 + [ANY] * 7,
        [
            pltpu.VMEM((LEVELS, TAPS * C, C), BF),
            pltpu.VMEM((LEVELS - 1, ROWS, C), BF),
            pltpu.VMEM((tiles * TILE, TAPS * C), BF),
            pltpu.VMEM((LEVELS, tiles * TILE, C), F32),
            pltpu.VMEM((ROWS, C), BF),
            pltpu.VMEM((ROWS, C), BF),
            pltpu.SemaphoreType.DMA((7,)),
        ],
        flops=5 * 10**9, nbytes=10 * 10**6,
    )(*operands)


def shift(axis_size, by):
    return [(i, (i + by) % axis_size) for i in range(axis_size)]


def step(maps, upstream, weights, neighbours):
    micro = maps.shape[0]
    section = lax.axis_index("section")
    core = lax.axis_index("core")
    patches = lax.axis_size("py") * lax.axis_size("core")
    patch = lax.axis_index("py") * lax.axis_size("core") + core
    npix = PIX * patches
    cores = jnp.stack([core, section]).astype(jnp.int32)

    sections = lax.axis_size("section")
    ways = [(2 * i + c, 2 * ((i + (1, -1)[c]) % sections) + c) for i in range(sections) for c in range(2)]
    near1 = lax.ppermute(lax.dynamic_slice_in_dim(weights[0], core * HALF, HALF), ("section", "core"), ways)
    near2 = lax.ppermute(lax.dynamic_slice_in_dim(weights[0], (1 - core) * HALF, HALF), ("section", "core"), ways)
    far = lax.ppermute(near1, ("section", "core"), ways)
    parts = []
    for block in (near1, near2, far):
        parts += [block, lax.ppermute(block, "core", shift(2, 1))]

    place = patch * PIX + jnp.arange(PIX, dtype=jnp.int32)
    offsets = jnp.mod(neighbours - place[None, :] + HALO, npix) - HALO
    offsets = jnp.pad(offsets.astype(BF).T, ((0, 0), (0, 128 - TAPS)))
    start = lax.dynamic_index_in_dim(maps, section, 0, keepdims=False)[0]
    top = lax.dynamic_index_in_dim(upstream, section, 0, keepdims=False)[0]
    own = jnp.concatenate([start, offsets, top], axis=1)
    edge = 2 * HALO
    send = functools.partial(lax.ppermute, axis_name=("py", "core"))
    m1a = send(own, perm=shift(patches, 1))
    m1b = send(own, perm=shift(patches, -1))
    m2a = send(own, perm=shift(patches, 2))
    m2b = send(own, perm=shift(patches, -2))
    m3a = send(own[PIX - edge:, :C + 128], perm=shift(patches, 3))
    m3b = send(own[:edge, :C + 128], perm=shift(patches, -3))

    *window, hot = prep_call(cores, m3a, m2a, m1a, own, m1b, m2b, m3b)
    out = stack_call(cores, *window, weights[0], *parts)

    mine = lax.all_to_all(out, "section", 0, 0, tiled=True)
    other = lax.ppermute(mine[:, :HROWS + PROWS], "core", shift(2, 1))
    chips = lax.axis_size("dp") * lax.axis_size("py")
    rows = (TAPS + 1) * C
    part, gin = call(
        grad_kernel,
        [jax.ShapeDtypeStruct((rows, 128), BF), jax.ShapeDtypeStruct((micro, PIX, C), BF)],
        [SMEM] + [VMEM] * 3,
        [
            pltpu.VMEM((2 * PROWS, micro * 128), BF),
            pltpu.VMEM((micro * 2 * PIX, C), BF),
            pltpu.VMEM((micro * 2 * PIX, 128), BF),
        ],
        flops=10**9, nbytes=2 * 10**6,
    )(cores, mine, other, hot)
    pieces = lax.all_to_all(part.reshape((chips, rows // chips, 128)), ("dp", "py"), 0, 0, tiled=True)
    total = call(
        sum_kernel, jax.ShapeDtypeStruct(pieces.shape, BF), [VMEM], nbytes=10**6,
    )(pieces)
    full = lax.all_to_all(total, ("dp", "py"), 0, 0, tiled=True).reshape((rows, 128))
    swapped = lax.ppermute(full, "core", shift(2, 1))
    summed = call(
        join_kernel, jax.ShapeDtypeStruct((TAPS * C, C), BF), [SMEM, VMEM, VMEM], nbytes=2 * 10**6,
    )(cores, full, swapped)
    return (gin[None, :, None], summed[None])


def solution(mesh):
    size = dict(mesh.shape)
    grid = (size["dp"], size["section"], size["patch"] // 2, 2)
    fine = Mesh(mesh.devices.reshape(grid), ("dp", "section", "py", "core"))
    patch = ("py", "core")
    in_specs = (
        P(None, "dp", patch, None),
        P(None, "dp", patch, None),
        P("section", None, None),
        P(None, patch),
    )
    out_specs = (P("section", None, "dp", patch, None), P("section", None, None))
    return jax.shard_map(step, mesh=fine, in_specs=in_specs, out_specs=out_specs, check_vma=False)
```

```python
import functools

import jax
import jax.numpy as jnp
from jax import lax
from jax.experimental import pallas as pl
from jax.experimental.pallas import tpu as pltpu
from jax.sharding import Mesh
from jax.sharding import PartitionSpec as P


HALO = 32
TAPS = 9
C = 256
PIX = 96
LEVELS = 4
REACH = 2 * LEVELS * HALO
TILE = 64
PAD = 32
WIN = PIX + 2 * REACH
ROWS = WIN + 2 * PAD
HALF = TAPS * C // 2
BF = jnp.bfloat16
F32 = jnp.float32
NT = (((1,), (1,)), ((), ()))

FWD_TILES = ((0, 9), (1, 9), (1, 8), (2, 8))
PRE_ROWS = ((224, 384), (192, 416), (160, 448), (128, 480))
BWD_TILES = ((4, 6), (3, 6), (3, 7), (2, 7))
OWN = REACH
HROWS, PROWS, GROWS = PIX, PIX + HALO, PIX
MSG = HROWS + PROWS + GROWS


def expand(gat, t, src, hot):
    rows = jnp.dot(hot, src, preferred_element_type=F32).astype(BF)
    dst = pl.ds(pl.multiple_of(t * TILE, TILE), TILE)
    gat[dst, :C] = src[PAD:PAD + TILE]
    for k in range(1, TAPS):
        gat[dst, k * C:(k + 1) * C] = rows[(k - 1) * TILE:k * TILE]


def expand_all(gat, first, last, src_ref, hot_ref, group):
    def one(t):
        expand(gat, t, src_ref[pl.ds(pl.multiple_of(t * TILE, TILE), 2 * TILE), :], hot_ref[t])

    def some(i, carry):
        for j in range(group):
            one(first + i * group + j)
        return carry

    whole = (last - first) // group
    if whole:
        lax.fori_loop(0, whole, some, 0)
    for t in range(first + whole * group, last):
        one(t)


def prep_kernel(ids_ref, m3a, m2a, m1a, own, m1b, m2b, m3b, h_ref, g_ref, s_ref, st_ref, gat_ref, pair_ref, off_buf):
    core = ids_ref[0]
    h_ref[:PAD, :] = jnp.zeros((PAD, C), BF)
    h_ref[ROWS - PAD:, :] = jnp.zeros((PAD, C), BF)
    g_ref[...] = jnp.zeros_like(g_ref)
    off_buf[:PAD, :] = jnp.zeros((PAD, 128), F32)
    off_buf[ROWS - PAD:, :] = jnp.zeros((PAD, 128), F32)
    at = PAD
    for piece in (m3a, m2a, m1a, own, m1b, m2b, m3b):
        n = piece.shape[0]
        h_ref[at:at + n, :] = piece[:, :C]
        off_buf[at:at + n, :] = piece[:, C:C + 128].astype(F32)
        if piece.shape[1] > C + 128:
            g_ref[at:at + n, :] = piece[:, C + 128:]
        at += n

    rel = (lax.broadcasted_iota(jnp.int32, (TILE, 128), 1)
           - lax.broadcasted_iota(jnp.int32, (TILE, 128), 0) - HALO).astype(F32)

    def build_s(t, carry):
        d = off_buf[pl.ds(pl.multiple_of(t * TILE + PAD, PAD), TILE), :]
        for k in range(1, TAPS):
            hit = rel == d[:, k:k + 1]
            s_ref[t, (k - 1) * TILE:k * TILE, :] = jnp.where(hit, 1.0, 0.0).astype(BF)
        return carry

    lax.fori_loop(0, FWD_TILES[0][1], build_s, 0)

    def build_st(t, carry):
        d = jnp.transpose(off_buf[pl.ds(pl.multiple_of(t * TILE, TILE), 128), :])
        for k in range(1, TAPS):
            hit = -rel == d[k:k + 1, :]
            st_ref[t, (k - 1) * TILE:k * TILE, :] = jnp.where(hit, 1.0, 0.0).astype(BF)
        return carry

    lax.fori_loop(BWD_TILES[3][0], BWD_TILES[3][1], build_st, 0)
    expand_all(gat_ref, *FWD_TILES[0], h_ref, s_ref, 3)

    start = pl.multiple_of(PAD + OWN - HALO - PIX * core, HALO)
    offt = jnp.transpose(off_buf[pl.ds(start, 2 * PROWS), :])
    apart = (lax.broadcasted_iota(jnp.int32, (2 * PIX, 2 * PROWS), 0)
             - lax.broadcasted_iota(jnp.int32, (2 * PIX, 2 * PROWS), 1) + HALO).astype(F32)
    for k in range(1, TAPS):
        pair_ref[k - 1] = jnp.where(apart == offt[k:k + 1, :], 1.0, 0.0).astype(BF)


def stack_kernel(ids_ref, h0, g_top, s_buf, st_buf, gat0, w_own, near_mine, near_other, far_mine, far_other,
                 out_ref, w_buf, h_buf, gat, der, pre_buf, g_buf, sems):
    core, section = ids_ref[0], ids_ref[1]
    left, right = lax.rem(section + 3, LEVELS), lax.rem(section + 1, LEVELS)
    far = w_buf.at[lax.rem(section + 2, LEVELS)]
    here = pl.ds(pl.multiple_of(core * HALF, HALF), HALF)
    there = pl.ds(pl.multiple_of((1 - core) * HALF, HALF), HALF)
    copies = []
    for n, (src, dst) in enumerate((
        (w_own, w_buf.at[section]),
        (near_mine, w_buf.at[jnp.where(core == 0, left, right)]),
        (near_other, w_buf.at[jnp.where(core == 0, right, left)]),
        (far_mine, far.at[here, :]),
        (far_other, far.at[there, :]),
    )):
        copies.append(pltpu.make_async_copy(src, dst, sems.at[n]))
        copies[-1].start()
    h_buf[...] = jnp.zeros_like(h_buf)
    pre_buf[...] = jnp.zeros_like(pre_buf)
    g_buf[...] = g_top[...]
    for copy in copies:
        copy.wait()

    for level in range(LEVELS):
        first, last = FWD_TILES[level]

        src = h0 if level == 0 else h_buf.at[level - 1]
        rows = gat0 if level == 0 else gat
        if level:
            expand_all(gat, first, last, src, s_buf, 3)
        lo, hi = first * TILE, last * TILE
        act = jnp.dot(rows[lo:hi, :], w_buf[level], preferred_element_type=F32)
        squash = jnp.tanh(act)
        der[level, lo:hi, :] = 1.0 - squash * squash
        if level + 1 < LEVELS:
            h_buf[level, PAD + lo:PAD + hi, :] = (src[PAD + lo:PAD + hi, :].astype(F32) + squash).astype(BF)
        out_ref[level, :HROWS, :] = src[PAD + OWN:PAD + OWN + PIX, :]

    for level in range(LEVELS - 1, -1, -1):
        lo, hi = PRE_ROWS[level]
        pre_buf[PAD + lo:PAD + hi, :] = (
            g_buf[PAD + lo:PAD + hi, :].astype(F32) * der[level, lo:hi, :]).astype(BF)
        first, last = BWD_TILES[level]

        expand_all(gat, first, last, pre_buf, st_buf, 3)
        lo, hi = first * TILE, last * TILE
        total = g_buf[PAD + lo:PAD + hi, :].astype(F32)
        for k in range(TAPS):
            total = total + lax.dot_general(gat[lo:hi, k * C:(k + 1) * C],
                                            w_buf[level, k * C:(k + 1) * C, :], NT,
                                            preferred_element_type=F32)
        g_buf[PAD + lo:PAD + hi, :] = total.astype(BF)
        start = pl.multiple_of(PAD + OWN - HALO + HALO * core, HALO)
        out_ref[level, HROWS:HROWS + PROWS, :] = pre_buf[pl.ds(start, PROWS), :]
        out_ref[level, HROWS + PROWS:, :] = g_buf[PAD + OWN:PAD + OWN + PIX, :]


def grad_kernel(core_ref, mine, other, hot, out_ref, gin_ref, p_buf, h_buf, t_buf):
    core = core_ref[0]
    micro = mine.shape[0]
    pair = 2 * PIX
    gin_ref[...] = mine[:, HROWS + PROWS:, :]
    for c in range(2):
        @pl.when(core == c)
        def _(c=c):
            both = (mine, other) if c == 0 else (other, mine)
            for m in range(micro):
                for n, ref in enumerate(both):
                    p_buf[n * PROWS:(n + 1) * PROWS, m * 128:(m + 1) * 128] = (
                        ref[m, HROWS:HROWS + PROWS, c * 128:(c + 1) * 128])
                    h_buf[m * pair + n * PIX:m * pair + (n + 1) * PIX, :] = ref[m, :HROWS, :]
    h_t = jnp.transpose(h_buf[...].astype(F32)).astype(BF)
    pre = p_buf[...]
    for k in range(TAPS):
        if k == 0:
            spread = pre[HALO:HALO + pair]
        else:
            spread = jnp.dot(hot[k - 1], pre, preferred_element_type=F32).astype(BF)
        for m in range(micro):
            t_buf[m * pair:(m + 1) * pair, :] = spread[:, m * 128:(m + 1) * 128]
        block = jnp.dot(h_t, t_buf[...], preferred_element_type=F32)
        out_ref[k * C:(k + 1) * C, :] = block.astype(BF)
    out_ref[TAPS * C:, :] = jnp.zeros((out_ref.shape[0] - TAPS * C, 128), BF)


def sum_kernel(x_ref, out_ref):
    total = jnp.sum(x_ref[...].astype(F32), axis=0).astype(BF)
    out_ref[...] = jnp.broadcast_to(total[None], out_ref.shape)


def join_kernel(core_ref, mine, other, out_ref):
    for c in range(2):
        @pl.when(core_ref[0] == c)
        def _(c=c):
            rows = out_ref.shape[0]
            out_ref[:, c * 128:(c + 1) * 128] = mine[:rows]
            out_ref[:, (1 - c) * 128:(2 - c) * 128] = other[:rows]


VMEM = pl.BlockSpec(memory_space=pltpu.VMEM)
SMEM = pl.BlockSpec(memory_space=pltpu.SMEM)
ANY = pl.BlockSpec(memory_space=pl.ANY)
INTERPRET = False


def call(kernel, out_shape, in_specs, scratch=(), flops=0, nbytes=0):
    many = isinstance(out_shape, (tuple, list))
    return pl.pallas_call(
        kernel,
        out_shape=out_shape,
        in_specs=in_specs,
        out_specs=[VMEM] * len(out_shape) if many else VMEM,
        scratch_shapes=list(scratch),
        interpret=INTERPRET,
        cost_estimate=pl.CostEstimate(flops=flops, bytes_accessed=nbytes, transcendentals=0),
        compiler_params=pltpu.CompilerParams(vmem_limit_bytes=28 << 20),
    )


def prep_call(*operands):
    tiles, hot = FWD_TILES[0][1], (TAPS - 1) * TILE
    return call(
        prep_kernel,
        [
            jax.ShapeDtypeStruct((ROWS, C), BF),
            jax.ShapeDtypeStruct((ROWS, C), BF),
            jax.ShapeDtypeStruct((tiles, hot, 2 * TILE), BF),
            jax.ShapeDtypeStruct((BWD_TILES[3][1], hot, 2 * TILE), BF),
            jax.ShapeDtypeStruct((tiles * TILE, TAPS * C), BF),
            jax.ShapeDtypeStruct((TAPS - 1, 2 * PIX, 2 * PROWS), BF),
        ],
        [SMEM] + [VMEM] * 7,
        [pltpu.VMEM((ROWS, 128), F32)],
        flops=10**9, nbytes=6 * 10**6,
    )(*operands)


def stack_call(*operands):
    tiles = FWD_TILES[0][1]
    return call(
        stack_kernel,
        jax.ShapeDtypeStruct((LEVELS, MSG, C), BF),
        [SMEM] + [VMEM] * 5 + [ANY] * 5,
        [
            pltpu.VMEM((LEVELS, TAPS * C, C), BF),
            pltpu.VMEM((LEVELS - 1, ROWS, C), BF),
            pltpu.VMEM((tiles * TILE, TAPS * C), BF),
            pltpu.VMEM((LEVELS, tiles * TILE, C), F32),
            pltpu.VMEM((ROWS, C), BF),
            pltpu.VMEM((ROWS, C), BF),
            pltpu.SemaphoreType.DMA((5,)),
        ],
        flops=5 * 10**9, nbytes=10 * 10**6,
    )(*operands)


def shift(axis_size, by):
    return [(i, (i + by) % axis_size) for i in range(axis_size)]


def step(maps, upstream, weights, neighbours):
    micro = maps.shape[0]
    section = lax.axis_index("section")
    core = lax.axis_index("core")
    patches = lax.axis_size("py") * lax.axis_size("core")
    patch = lax.axis_index("py") * lax.axis_size("core") + core
    npix = PIX * patches
    cores = jnp.stack([core, section]).astype(jnp.int32)

    sections = lax.axis_size("section")
    ways = [(2 * i + c, 2 * ((i + (1, -1)[c]) % sections) + c) for i in range(sections) for c in range(2)]
    near = lax.ppermute(weights[0], ("section", "core"), ways)
    half = lax.dynamic_slice_in_dim(near, core * HALF, HALF)
    far = lax.ppermute(half, ("section", "core"), ways)
    parts = []
    for block in (near, far):
        parts += [block, lax.ppermute(block, "core", shift(2, 1))]

    place = patch * PIX + jnp.arange(PIX, dtype=jnp.int32)
    offsets = jnp.mod(neighbours - place[None, :] + HALO, npix) - HALO
    offsets = jnp.pad(offsets.astype(BF).T, ((0, 0), (0, 128 - TAPS)))
    start = lax.dynamic_index_in_dim(maps, section, 0, keepdims=False)[0]
    top = lax.dynamic_index_in_dim(upstream, section, 0, keepdims=False)[0]
    own = jnp.concatenate([start, offsets, top], axis=1)
    edge = 2 * HALO
    send = functools.partial(lax.ppermute, axis_name=("py", "core"))
    m1a = send(own, perm=shift(patches, 1))
    m1b = send(own, perm=shift(patches, -1))
    m2a = send(own, perm=shift(patches, 2))
    m2b = send(own, perm=shift(patches, -2))
    m3a = send(own[PIX - edge:, :C + 128], perm=shift(patches, 3))
    m3b = send(own[:edge, :C + 128], perm=shift(patches, -3))

    *window, hot = prep_call(cores, m3a, m2a, m1a, own, m1b, m2b, m3b)
    out = stack_call(cores, *window, weights[0], *parts)

    mine = lax.all_to_all(out, "section", 0, 0, tiled=True)
    other = lax.ppermute(mine[:, :HROWS + PROWS], "core", shift(2, 1))
    chips = lax.axis_size("dp") * lax.axis_size("py")
    rows = (TAPS + 1) * C
    part, gin = call(
        grad_kernel,
        [jax.ShapeDtypeStruct((rows, 128), BF), jax.ShapeDtypeStruct((micro, PIX, C), BF)],
        [SMEM] + [VMEM] * 3,
        [
            pltpu.VMEM((2 * PROWS, micro * 128), BF),
            pltpu.VMEM((micro * 2 * PIX, C), BF),
            pltpu.VMEM((micro * 2 * PIX, 128), BF),
        ],
        flops=10**9, nbytes=2 * 10**6,
    )(cores, mine, other, hot)
    pieces = lax.all_to_all(part.reshape((chips, rows // chips, 128)), ("dp", "py"), 0, 0, tiled=True)
    total = call(
        sum_kernel, jax.ShapeDtypeStruct(pieces.shape, BF), [VMEM], nbytes=10**6,
    )(pieces)
    full = lax.all_to_all(total, ("dp", "py"), 0, 0, tiled=True).reshape((rows, 128))
    swapped = lax.ppermute(full, "core", shift(2, 1))
    summed = call(
        join_kernel, jax.ShapeDtypeStruct((TAPS * C, C), BF), [SMEM, VMEM, VMEM], nbytes=2 * 10**6,
    )(cores, full, swapped)
    return (gin[None, :, None], summed[None])


def solution(mesh):
    size = dict(mesh.shape)
    grid = (size["dp"], size["section"], size["patch"] // 2, 2)
    fine = Mesh(mesh.devices.reshape(grid), ("dp", "section", "py", "core"))
    patch = ("py", "core")
    in_specs = (
        P(None, "dp", patch, None),
        P(None, "dp", patch, None),
        P("section", None, None),
        P(None, patch),
    )
    out_specs = (P("section", None, "dp", patch, None), P("section", None, None))
    return jax.shard_map(step, mesh=fine, in_specs=in_specs, out_specs=out_specs, check_vma=False)
```

```python
import functools

import jax
import jax.numpy as jnp
from jax import lax
from jax.experimental import pallas as pl
from jax.experimental.pallas import tpu as pltpu
from jax.sharding import Mesh
from jax.sharding import PartitionSpec as P


HALO = 32
TAPS = 9
C = 256
PIX = 96
LEVELS = 4
REACH = 2 * LEVELS * HALO
TILE = 64
PAD = 32
WIN = PIX + 2 * REACH
ROWS = WIN + 2 * PAD
HALF = TAPS * C // 2
BF = jnp.bfloat16
F32 = jnp.float32
NT = (((1,), (1,)), ((), ()))

FWD_TILES = ((0, 9), (1, 9), (1, 8), (2, 8))
PRE_ROWS = ((224, 384), (192, 416), (160, 448), (128, 480))
BWD_TILES = ((4, 6), (3, 6), (3, 7), (2, 7))
EDGE = 2 * HALO
OFF = 16
OWN = REACH
HROWS, PROWS, GROWS = PIX, PIX + HALO, PIX
MSG = HROWS + PROWS + GROWS


def expand(gat, t, src, hot):
    rows = jnp.dot(hot, src, preferred_element_type=F32).astype(BF)
    dst = pl.ds(pl.multiple_of(t * TILE, TILE), TILE)
    gat[dst, :C] = src[PAD:PAD + TILE]
    for k in range(1, TAPS):
        gat[dst, k * C:(k + 1) * C] = rows[(k - 1) * TILE:k * TILE]


def expand_all(gat, first, last, src_ref, hot_ref, group):
    def one(t):
        expand(gat, t, src_ref[pl.ds(pl.multiple_of(t * TILE, TILE), 2 * TILE), :], hot_ref[t])

    def some(i, carry):
        for j in range(group):
            one(first + i * group + j)
        return carry

    whole = (last - first) // group
    if whole:
        lax.fori_loop(0, whole, some, 0)
    for t in range(first + whole * group, last):
        one(t)


def pack_kernel(npix, ids_ref, maps, upstream, neighbours, own, to2a, to2b, to3a, to3b, off_buf):
    start, top = maps[0, 0], upstream[0, 0]
    place = ids_ref[2] * PIX + lax.broadcasted_iota(jnp.int32, (TAPS, PIX), 1)
    offsets = neighbours[...] - place + HALO
    offsets = jnp.where(offsets < 0, offsets + npix, offsets)
    offsets = jnp.where(offsets >= npix, offsets - npix, offsets) - HALO
    off_buf[...] = jnp.zeros_like(off_buf)
    off_buf[:TAPS, :PIX] = offsets.astype(F32)
    tail = off_buf[...].astype(BF)
    for ref, rows in ((own, (start, top)), (to2a, (start, top[PIX - HALO:])), (to2b, (start, top[:HALO])),
                      (to3a, (start[PIX - EDGE:],)), (to3b, (start[:EDGE],))):
        at = 0
        for value in (*rows, tail):
            ref[at:at + value.shape[0], :] = value
            at += value.shape[0]


def pack_call(ids, maps, upstream, neighbours):
    npix = PIX * lax.axis_size("py") * lax.axis_size("core")
    mine = pl.BlockSpec((1, 1, PIX, C), lambda i, ids: (ids[1], 0, 0, 0))
    rows = [2 * PIX + OFF, PIX + HALO + OFF, PIX + HALO + OFF, EDGE + OFF, EDGE + OFF]
    return pl.pallas_call(
        functools.partial(pack_kernel, npix),
        grid_spec=pltpu.PrefetchScalarGridSpec(
            num_scalar_prefetch=1,
            grid=(1,),
            in_specs=[mine, mine, pl.BlockSpec((TAPS, PIX), lambda i, ids: (0, 0))],
            out_specs=[pl.BlockSpec((n, C), lambda i, ids: (0, 0)) for n in rows],
            scratch_shapes=[pltpu.VMEM((OFF, C), F32)],
        ),
        out_shape=[jax.ShapeDtypeStruct((n, C), BF) for n in rows],
        interpret=INTERPRET,
        cost_estimate=pl.CostEstimate(flops=0, bytes_accessed=10**6, transcendentals=0),
    )(ids, maps, upstream, neighbours)


def prep_kernel(ids_ref, m3a, m2a, m1a, own, m1b, m2b, m3b, w_own, near_mine, near_other,
                h_ref, g_ref, s_ref, st_ref, gat_ref, pair_ref, w_ref, off_buf, sems):
    core, section = ids_ref[0], ids_ref[1]
    left, right = lax.rem(section + 3, LEVELS), lax.rem(section + 1, LEVELS)
    copies = []
    for n, (src, level) in enumerate((
        (w_own, section),
        (near_mine, jnp.where(core == 0, left, right)),
        (near_other, jnp.where(core == 0, right, left)),
    )):
        copies.append(pltpu.make_async_copy(src, w_ref.at[level], sems.at[n]))
        copies[-1].start()
    h_ref[:PAD, :] = jnp.zeros((PAD, C), BF)
    h_ref[ROWS - PAD:, :] = jnp.zeros((PAD, C), BF)
    g_ref[...] = jnp.zeros_like(g_ref)
    off_buf[:PAD, :] = jnp.zeros((PAD, 128), F32)
    off_buf[ROWS - PAD:, :] = jnp.zeros((PAD, 128), F32)
    at = PAD
    shapes = ((EDGE, PIX - EDGE, 0, 0), (PIX, 0, HALO, PIX - HALO), (PIX, 0, PIX, 0), (PIX, 0, PIX, 0),
              (PIX, 0, PIX, 0), (PIX, 0, HALO, 0), (EDGE, 0, 0, 0))
    for piece, (n, first, n_top, first_top) in zip((m3a, m2a, m1a, own, m1b, m2b, m3b), shapes):
        h_ref[at:at + n, :] = piece[:n, :]
        if n_top:
            place = at + first_top
            g_ref[place:place + n_top, :] = piece[n:n + n_top, :]
        off_t = jnp.transpose(piece[n + n_top:, :128].astype(F32))
        off_buf[at:at + n, :OFF] = off_t[first:first + n]
        at += n

    rel = (lax.broadcasted_iota(jnp.int32, (TILE, 128), 1)
           - lax.broadcasted_iota(jnp.int32, (TILE, 128), 0) - HALO).astype(F32)

    def build_s(t, carry):
        d = off_buf[pl.ds(pl.multiple_of(t * TILE + PAD, PAD), TILE), :]
        for k in range(1, TAPS):
            hit = rel == d[:, k:k + 1]
            s_ref[t, (k - 1) * TILE:k * TILE, :] = jnp.where(hit, 1.0, 0.0).astype(BF)
        return carry

    lax.fori_loop(0, FWD_TILES[0][1], build_s, 0)

    def build_st(t, carry):
        d = jnp.transpose(off_buf[pl.ds(pl.multiple_of(t * TILE, TILE), 128), :])
        for k in range(1, TAPS):
            hit = -rel == d[k:k + 1, :]
            st_ref[t, (k - 1) * TILE:k * TILE, :] = jnp.where(hit, 1.0, 0.0).astype(BF)
        return carry

    lax.fori_loop(BWD_TILES[3][0], BWD_TILES[3][1], build_st, 0)
    expand_all(gat_ref, *FWD_TILES[0], h_ref, s_ref, 3)

    start = pl.multiple_of(PAD + OWN - HALO - PIX * core, HALO)
    offt = jnp.transpose(off_buf[pl.ds(start, 2 * PROWS), :])
    apart = (lax.broadcasted_iota(jnp.int32, (2 * PIX, 2 * PROWS), 0)
             - lax.broadcasted_iota(jnp.int32, (2 * PIX, 2 * PROWS), 1) + HALO).astype(F32)
    for k in range(1, TAPS):
        pair_ref[k - 1] = jnp.where(apart == offt[k:k + 1, :], 1.0, 0.0).astype(BF)
    for copy in copies:
        copy.wait()


def stack_kernel(ids_ref, h0, g_top, s_buf, st_buf, gat0, w_in, far_mine, far_other,
                 out_ref, w_buf, h_buf, gat, der, pre_buf, g_buf, sems):
    core, section = ids_ref[0], ids_ref[1]
    del w_in
    copies = []
    for n, (src, half) in enumerate(((far_mine, core), (far_other, 1 - core))):
        rows = pl.ds(pl.multiple_of(half * HALF, HALF), HALF)
        copies.append(pltpu.make_async_copy(src, w_buf.at[lax.rem(section + 2, LEVELS), rows, :], sems.at[n]))
        copies[-1].start()
    h_buf[...] = jnp.zeros_like(h_buf)
    pre_buf[...] = jnp.zeros_like(pre_buf)
    g_buf[...] = g_top[...]
    for copy in copies:
        copy.wait()

    for level in range(LEVELS):
        first, last = FWD_TILES[level]

        src = h0 if level == 0 else h_buf.at[level - 1]
        rows = gat0 if level == 0 else gat
        if level:
            expand_all(gat, first, last, src, s_buf, 3)
        lo, hi = first * TILE, last * TILE
        act = jnp.dot(rows[lo:hi, :], w_buf[level], preferred_element_type=F32)
        squash = jnp.tanh(act)
        der[level, lo:hi, :] = 1.0 - squash * squash
        if level + 1 < LEVELS:
            h_buf[level, PAD + lo:PAD + hi, :] = (src[PAD + lo:PAD + hi, :].astype(F32) + squash).astype(BF)
        out_ref[level, :HROWS, :] = src[PAD + OWN:PAD + OWN + PIX, :]

    for level in range(LEVELS - 1, -1, -1):
        lo, hi = PRE_ROWS[level]
        pre_buf[PAD + lo:PAD + hi, :] = (
            g_buf[PAD + lo:PAD + hi, :].astype(F32) * der[level, lo:hi, :]).astype(BF)
        first, last = BWD_TILES[level]

        expand_all(gat, first, last, pre_buf, st_buf, 3)
        lo, hi = first * TILE, last * TILE
        total = g_buf[PAD + lo:PAD + hi, :].astype(F32)
        for k in range(TAPS):
            total = total + lax.dot_general(gat[lo:hi, k * C:(k + 1) * C],
                                            w_buf[level, k * C:(k + 1) * C, :], NT,
                                            preferred_element_type=F32)
        g_buf[PAD + lo:PAD + hi, :] = total.astype(BF)
        start = pl.multiple_of(PAD + OWN - HALO + HALO * core, HALO)
        out_ref[level, HROWS:HROWS + PROWS, :] = pre_buf[pl.ds(start, PROWS), :]
        out_ref[level, HROWS + PROWS:, :] = g_buf[PAD + OWN:PAD + OWN + PIX, :]


def grad_kernel(core_ref, mine, other, hot, out_ref, gin_ref, p_buf, h_buf, t_buf):
    core = core_ref[0]
    micro = mine.shape[0]
    pair = 2 * PIX
    gin_ref[...] = mine[:, HROWS + PROWS:, :]
    for c in range(2):
        @pl.when(core == c)
        def _(c=c):
            both = (mine, other) if c == 0 else (other, mine)
            for m in range(micro):
                for n, ref in enumerate(both):
                    p_buf[n * PROWS:(n + 1) * PROWS, m * 128:(m + 1) * 128] = (
                        ref[m, HROWS:HROWS + PROWS, c * 128:(c + 1) * 128])
                    h_buf[m * pair + n * PIX:m * pair + (n + 1) * PIX, :] = ref[m, :HROWS, :]
    h_t = jnp.transpose(h_buf[...].astype(F32)).astype(BF)
    pre = p_buf[...]
    for k in range(TAPS):
        if k == 0:
            spread = pre[HALO:HALO + pair]
        else:
            spread = jnp.dot(hot[k - 1], pre, preferred_element_type=F32).astype(BF)
        for m in range(micro):
            t_buf[m * pair:(m + 1) * pair, :] = spread[:, m * 128:(m + 1) * 128]
        block = jnp.dot(h_t, t_buf[...], preferred_element_type=F32)
        out_ref[k * C:(k + 1) * C, :] = block.astype(BF)
    out_ref[TAPS * C:, :] = jnp.zeros((out_ref.shape[0] - TAPS * C, 128), BF)


def sum_kernel(x_ref, out_ref):
    total = jnp.sum(x_ref[...].astype(F32), axis=0).astype(BF)
    out_ref[...] = jnp.broadcast_to(total[None], out_ref.shape)


def join_kernel(core_ref, mine, other, out_ref):
    for c in range(2):
        @pl.when(core_ref[0] == c)
        def _(c=c):
            rows = out_ref.shape[0]
            out_ref[:, c * 128:(c + 1) * 128] = mine[:rows]
            out_ref[:, (1 - c) * 128:(2 - c) * 128] = other[:rows]


VMEM = pl.BlockSpec(memory_space=pltpu.VMEM)
SMEM = pl.BlockSpec(memory_space=pltpu.SMEM)
ANY = pl.BlockSpec(memory_space=pl.ANY)
INTERPRET = False


def call(kernel, out_shape, in_specs, scratch=(), flops=0, nbytes=0, aliases=None):
    many = isinstance(out_shape, (tuple, list))
    return pl.pallas_call(
        kernel,
        out_shape=out_shape,
        in_specs=in_specs,
        out_specs=[VMEM] * len(out_shape) if many else VMEM,
        scratch_shapes=list(scratch),
        interpret=INTERPRET,
        input_output_aliases=aliases or {},
        cost_estimate=pl.CostEstimate(flops=flops, bytes_accessed=nbytes, transcendentals=0),
        compiler_params=pltpu.CompilerParams(vmem_limit_bytes=28 << 20),
    )


def prep_call(*operands):
    tiles, hot = FWD_TILES[0][1], (TAPS - 1) * TILE
    return call(
        prep_kernel,
        [
            jax.ShapeDtypeStruct((ROWS, C), BF),
            jax.ShapeDtypeStruct((ROWS, C), BF),
            jax.ShapeDtypeStruct((tiles, hot, 2 * TILE), BF),
            jax.ShapeDtypeStruct((BWD_TILES[3][1], hot, 2 * TILE), BF),
            jax.ShapeDtypeStruct((tiles * TILE, TAPS * C), BF),
            jax.ShapeDtypeStruct((TAPS - 1, 2 * PIX, 2 * PROWS), BF),
            jax.ShapeDtypeStruct((LEVELS, TAPS * C, C), BF),
        ],
        [SMEM] + [VMEM] * 7 + [ANY] * 3,
        [pltpu.VMEM((ROWS, 128), F32), pltpu.SemaphoreType.DMA((3,))],
        flops=10**9, nbytes=12 * 10**6,
    )(*operands)


def stack_call(*operands):
    tiles = FWD_TILES[0][1]
    return call(
        stack_kernel,
        [jax.ShapeDtypeStruct((LEVELS, MSG, C), BF), jax.ShapeDtypeStruct((LEVELS, TAPS * C, C), BF)],
        [SMEM] + [VMEM] * 6 + [ANY] * 2,
        [
            pltpu.VMEM((LEVELS - 1, ROWS, C), BF),
            pltpu.VMEM((tiles * TILE, TAPS * C), BF),
            pltpu.VMEM((LEVELS, tiles * TILE, C), F32),
            pltpu.VMEM((ROWS, C), BF),
            pltpu.VMEM((ROWS, C), BF),
            pltpu.SemaphoreType.DMA((2,)),
        ],
        flops=5 * 10**9, nbytes=10 * 10**6, aliases={6: 1},
    )(*operands)


def shift(axis_size, by):
    return [(i, (i + by) % axis_size) for i in range(axis_size)]


def step(maps, upstream, weights, neighbours):
    micro = maps.shape[0]
    section = lax.axis_index("section")
    core = lax.axis_index("core")
    patches = lax.axis_size("py") * lax.axis_size("core")
    patch = lax.axis_index("py") * lax.axis_size("core") + core
    cores = jnp.stack([core, section, patch]).astype(jnp.int32)

    sections = lax.axis_size("section")
    ways = [(2 * i + c, 2 * ((i + (1, -1)[c]) % sections) + c) for i in range(sections) for c in range(2)]
    near = lax.ppermute(weights[0], ("section", "core"), ways)
    half = lax.dynamic_slice_in_dim(near, core * HALF, HALF)
    far = lax.ppermute(half, ("section", "core"), ways)
    near_other = lax.ppermute(near, "core", shift(2, 1))
    far_other = lax.ppermute(far, "core", shift(2, 1))

    own, to2a, to2b, to3a, to3b = pack_call(cores, maps, upstream, neighbours)
    send = functools.partial(lax.ppermute, axis_name=("py", "core"))
    m1a = send(own, perm=shift(patches, 1))
    m1b = send(own, perm=shift(patches, -1))
    m2a = send(to2a, perm=shift(patches, 2))
    m2b = send(to2b, perm=shift(patches, -2))
    m3a = send(to3a, perm=shift(patches, 3))
    m3b = send(to3b, perm=shift(patches, -3))

    h0, g_top, s_hot, st_hot, gat0, hot, w_all = prep_call(
        cores, m3a, m2a, m1a, own, m1b, m2b, m3b, weights[0], near, near_other)
    out, _ = stack_call(cores, h0, g_top, s_hot, st_hot, gat0, w_all, far, far_other)

    mine = lax.all_to_all(out, "section", 0, 0, tiled=True)
    other = lax.ppermute(mine[:, :HROWS + PROWS], "core", shift(2, 1))
    chips = lax.axis_size("dp") * lax.axis_size("py")
    rows = (TAPS + 1) * C
    part, gin = call(
        grad_kernel,
        [jax.ShapeDtypeStruct((rows, 128), BF), jax.ShapeDtypeStruct((micro, PIX, C), BF)],
        [SMEM] + [VMEM] * 3,
        [
            pltpu.VMEM((2 * PROWS, micro * 128), BF),
            pltpu.VMEM((micro * 2 * PIX, C), BF),
            pltpu.VMEM((micro * 2 * PIX, 128), BF),
        ],
        flops=10**9, nbytes=2 * 10**6,
    )(cores, mine, other, hot)
    pieces = lax.all_to_all(part.reshape((chips, rows // chips, 128)), ("dp", "py"), 0, 0, tiled=True)
    total = call(
        sum_kernel, jax.ShapeDtypeStruct(pieces.shape, BF), [VMEM], nbytes=10**6,
    )(pieces)
    full = lax.all_to_all(total, ("dp", "py"), 0, 0, tiled=True).reshape((rows, 128))
    swapped = lax.ppermute(full, "core", shift(2, 1))
    block = pl.BlockSpec((C, 128), lambda i: (i, 0))
    summed = pl.pallas_call(
        join_kernel,
        grid=(TAPS,),
        out_shape=jax.ShapeDtypeStruct((TAPS * C, C), BF),
        in_specs=[SMEM, block, block],
        out_specs=pl.BlockSpec((C, C), lambda i: (i, 0)),
        interpret=INTERPRET,
    )(cores, full, swapped)
    return (gin[None, :, None], summed[None])


def solution(mesh):
    size = dict(mesh.shape)
    grid = (size["dp"], size["section"], size["patch"] // 2, 2)
    fine = Mesh(mesh.devices.reshape(grid), ("dp", "section", "py", "core"))
    patch = ("py", "core")
    in_specs = (
        P(None, "dp", patch, None),
        P(None, "dp", patch, None),
        P("section", None, None),
        P(None, patch),
    )
    out_specs = (P("section", None, "dp", patch, None), P("section", None, None))
    return jax.shard_map(step, mesh=fine, in_specs=in_specs, out_specs=out_specs, check_vma=False)
```

```python
import functools

import jax
import jax.numpy as jnp
from jax import lax
from jax.experimental import pallas as pl
from jax.experimental.pallas import tpu as pltpu
from jax.sharding import Mesh
from jax.sharding import PartitionSpec as P


HALO = 32
TAPS = 9
C = 256
PIX = 96
LEVELS = 4
REACH = 2 * LEVELS * HALO
TILE = 64
PAD = 32
WIN = PIX + 2 * REACH
ROWS = WIN + 2 * PAD
HALF = TAPS * C // 2
BF = jnp.bfloat16
F32 = jnp.float32
NT = (((1,), (1,)), ((), ()))

FWD_ROWS = ((32, 576), (64, 544), (96, 512), (128, 480))
FWD_TILES = ((0, 9), (1, 9), (1, 8), (2, 8))
PRE_ROWS = ((224, 384), (192, 416), (160, 448), (128, 480))
BWD_ROWS = ((256, 352), (224, 384), (192, 416), (160, 448))
BWD_TILES = ((4, 6), (3, 6), (3, 7), (2, 7))
EDGE = 2 * HALO
OFF = 16
OWN = REACH
HROWS, PROWS, GROWS = PIX, PIX + HALO, PIX
MSG = HROWS + PROWS + GROWS


def expand(gat, t, src, hot):
    rows = jnp.dot(hot, src, preferred_element_type=F32).astype(BF)
    dst = pl.ds(pl.multiple_of(t * TILE, TILE), TILE)
    gat[dst, :C] = src[PAD:PAD + TILE]
    for k in range(1, TAPS):
        gat[dst, k * C:(k + 1) * C] = rows[(k - 1) * TILE:k * TILE]


def expand_all(gat, first, last, src_ref, hot_ref, group):
    def one(t):
        expand(gat, t, src_ref[pl.ds(pl.multiple_of(t * TILE, TILE), 2 * TILE), :], hot_ref[t])

    def some(i, carry):
        for j in range(group):
            one(first + i * group + j)
        return carry

    whole = (last - first) // group
    if whole:
        lax.fori_loop(0, whole, some, 0)
    for t in range(first + whole * group, last):
        one(t)


def pack_kernel(npix, ids_ref, maps, upstream, neighbours, own, to2a, to2b, to3a, to3b, off_buf):
    start, top = maps[0, 0], upstream[0, 0]
    place = ids_ref[2] * PIX + lax.broadcasted_iota(jnp.int32, (TAPS, PIX), 1)
    offsets = neighbours[...] - place + HALO
    offsets = jnp.where(offsets < 0, offsets + npix, offsets)
    offsets = jnp.where(offsets >= npix, offsets - npix, offsets) - HALO
    off_buf[...] = jnp.zeros_like(off_buf)
    off_buf[:TAPS, :PIX] = offsets.astype(F32)
    tail = off_buf[...].astype(BF)
    for ref, rows in ((own, (start, top)), (to2a, (start, top[PIX - HALO:])), (to2b, (start, top[:HALO])),
                      (to3a, (start[PIX - EDGE:],)), (to3b, (start[:EDGE],))):
        at = 0
        for value in (*rows, tail):
            ref[at:at + value.shape[0], :] = value
            at += value.shape[0]


def pack_call(ids, maps, upstream, neighbours):
    npix = PIX * lax.axis_size("py") * lax.axis_size("core")
    mine = pl.BlockSpec((1, 1, PIX, C), lambda i, ids: (ids[1], 0, 0, 0))
    rows = [2 * PIX + OFF, PIX + HALO + OFF, PIX + HALO + OFF, EDGE + OFF, EDGE + OFF]
    return pl.pallas_call(
        functools.partial(pack_kernel, npix),
        grid_spec=pltpu.PrefetchScalarGridSpec(
            num_scalar_prefetch=1,
            grid=(1,),
            in_specs=[mine, mine, pl.BlockSpec((TAPS, PIX), lambda i, ids: (0, 0))],
            out_specs=[pl.BlockSpec((n, C), lambda i, ids: (0, 0)) for n in rows],
            scratch_shapes=[pltpu.VMEM((OFF, C), F32)],
        ),
        out_shape=[jax.ShapeDtypeStruct((n, C), BF) for n in rows],
        interpret=INTERPRET,
        cost_estimate=pl.CostEstimate(flops=0, bytes_accessed=10**6, transcendentals=0),
    )(ids, maps, upstream, neighbours)


def prep_kernel(ids_ref, m3a, m2a, m1a, own, m1b, m2b, m3b, w_own, near_mine,
                h_ref, g_ref, s_ref, st_ref, gat_ref, pair_ref, w_ref, off_buf, sems):
    core, section = ids_ref[0], ids_ref[1]
    left, right = lax.rem(section + 3, LEVELS), lax.rem(section + 1, LEVELS)
    copies = []
    for n, (src, level) in enumerate((
        (w_own, section),
        (near_mine, jnp.where(core == 0, left, right)),
    )):
        copies.append(pltpu.make_async_copy(src, w_ref.at[level], sems.at[n]))
        copies[-1].start()
    h_ref[:PAD, :] = jnp.zeros((PAD, C), BF)
    h_ref[ROWS - PAD:, :] = jnp.zeros((PAD, C), BF)
    g_ref[...] = jnp.zeros_like(g_ref)
    off_buf[:PAD, :] = jnp.zeros((PAD, 128), F32)
    off_buf[ROWS - PAD:, :] = jnp.zeros((PAD, 128), F32)
    at = PAD
    shapes = ((EDGE, PIX - EDGE, 0, 0), (PIX, 0, HALO, PIX - HALO), (PIX, 0, PIX, 0), (PIX, 0, PIX, 0),
              (PIX, 0, PIX, 0), (PIX, 0, HALO, 0), (EDGE, 0, 0, 0))
    for piece, (n, first, n_top, first_top) in zip((m3a, m2a, m1a, own, m1b, m2b, m3b), shapes):
        h_ref[at:at + n, :] = piece[:n, :]
        if n_top:
            place = at + first_top
            g_ref[place:place + n_top, :] = piece[n:n + n_top, :]
        off_t = jnp.transpose(piece[n + n_top:, :128].astype(F32))
        off_buf[at:at + n, :OFF] = off_t[first:first + n]
        at += n

    rel = (lax.broadcasted_iota(jnp.int32, (TILE, 128), 1)
           - lax.broadcasted_iota(jnp.int32, (TILE, 128), 0) - HALO).astype(F32)

    def build_s(t, carry):
        d = off_buf[pl.ds(pl.multiple_of(t * TILE + PAD, PAD), TILE), :]
        for k in range(1, TAPS):
            hit = rel == d[:, k:k + 1]
            s_ref[t, (k - 1) * TILE:k * TILE, :] = jnp.where(hit, 1.0, 0.0).astype(BF)
        return carry

    lax.fori_loop(0, FWD_TILES[0][1], build_s, 0)

    def build_st(t, carry):
        d = jnp.transpose(off_buf[pl.ds(pl.multiple_of(t * TILE, TILE), 128), :])
        for k in range(1, TAPS):
            hit = -rel == d[k:k + 1, :]
            st_ref[t, (k - 1) * TILE:k * TILE, :] = jnp.where(hit, 1.0, 0.0).astype(BF)
        return carry

    lax.fori_loop(BWD_TILES[3][0], BWD_TILES[3][1], build_st, 0)
    expand_all(gat_ref, *FWD_TILES[0], h_ref, s_ref, 3)

    start = pl.multiple_of(PAD + OWN - HALO - PIX * core, HALO)
    offt = jnp.transpose(off_buf[pl.ds(start, 2 * PROWS), :])
    apart = (lax.broadcasted_iota(jnp.int32, (2 * PIX, 2 * PROWS), 0)
             - lax.broadcasted_iota(jnp.int32, (2 * PIX, 2 * PROWS), 1) + HALO).astype(F32)
    for k in range(1, TAPS):
        pair_ref[k - 1] = jnp.where(apart == offt[k:k + 1, :], 1.0, 0.0).astype(BF)
    for copy in copies:
        copy.wait()


def stack_kernel(ids_ref, h0, g_top, s_buf, st_buf, gat0, w_in, near_other, far_mine, far_other,
                 out_ref, w_buf, h_buf, gat, der, pre_buf, g_buf, sems):
    core, section = ids_ref[0], ids_ref[1]
    del w_in
    far = w_buf.at[lax.rem(section + 2, LEVELS)]
    copies = []
    for n, (src, dst) in enumerate((
        (near_other, w_buf.at[lax.rem(section + 1 + 2 * core, LEVELS)]),
        (far_mine, far.at[pl.ds(pl.multiple_of(core * HALF, HALF), HALF), :]),
        (far_other, far.at[pl.ds(pl.multiple_of((1 - core) * HALF, HALF), HALF), :]),
    )):
        copies.append(pltpu.make_async_copy(src, dst, sems.at[n]))
        copies[-1].start()
    h_buf[...] = jnp.zeros_like(h_buf)
    pre_buf[...] = jnp.zeros_like(pre_buf)
    g_buf[...] = g_top[...]
    for copy in copies:
        copy.wait()

    for level in range(LEVELS):
        first, last = FWD_TILES[level]

        src = h0 if level == 0 else h_buf.at[level - 1]
        rows = gat0 if level == 0 else gat
        if level:
            expand_all(gat, first, last, src, s_buf, 3)
        lo, hi = FWD_ROWS[level]
        act = jnp.dot(rows[lo:hi, :], w_buf[level], preferred_element_type=F32)
        squash = jnp.tanh(act)
        der[level, lo:hi, :] = 1.0 - squash * squash
        if level + 1 < LEVELS:
            h_buf[level, PAD + lo:PAD + hi, :] = (src[PAD + lo:PAD + hi, :].astype(F32) + squash).astype(BF)
        out_ref[level, :HROWS, :] = src[PAD + OWN:PAD + OWN + PIX, :]

    for level in range(LEVELS - 1, -1, -1):
        lo, hi = PRE_ROWS[level]
        pre_buf[PAD + lo:PAD + hi, :] = (
            g_buf[PAD + lo:PAD + hi, :].astype(F32) * der[level, lo:hi, :]).astype(BF)
        first, last = BWD_TILES[level]

        expand_all(gat, first, last, pre_buf, st_buf, 3)
        lo, hi = BWD_ROWS[level]
        total = g_buf[PAD + lo:PAD + hi, :].astype(F32)
        for k in range(TAPS):
            total = total + lax.dot_general(gat[lo:hi, k * C:(k + 1) * C],
                                            w_buf[level, k * C:(k + 1) * C, :], NT,
                                            preferred_element_type=F32)
        g_buf[PAD + lo:PAD + hi, :] = total.astype(BF)
        start = pl.multiple_of(PAD + OWN - HALO + HALO * core, HALO)
        out_ref[level, HROWS:HROWS + PROWS, :] = pre_buf[pl.ds(start, PROWS), :]
        out_ref[level, HROWS + PROWS:, :] = g_buf[PAD + OWN:PAD + OWN + PIX, :]


def grad_kernel(core_ref, mine, other, hot, out_ref, gin_ref, p_buf, h_buf, t_buf):
    core = core_ref[0]
    micro = mine.shape[0]
    pair = 2 * PIX
    gin_ref[...] = mine[:, HROWS + PROWS:, :]
    for c in range(2):
        @pl.when(core == c)
        def _(c=c):
            both = (mine, other) if c == 0 else (other, mine)
            for m in range(micro):
                for n, ref in enumerate(both):
                    p_buf[n * PROWS:(n + 1) * PROWS, m * 128:(m + 1) * 128] = (
                        ref[m, HROWS:HROWS + PROWS, c * 128:(c + 1) * 128])
                    h_buf[m * pair + n * PIX:m * pair + (n + 1) * PIX, :] = ref[m, :HROWS, :]
    h_t = jnp.transpose(h_buf[...].astype(F32)).astype(BF)
    pre = p_buf[...]
    for k in range(TAPS):
        if k == 0:
            spread = pre[HALO:HALO + pair]
        else:
            spread = jnp.dot(hot[k - 1], pre, preferred_element_type=F32).astype(BF)
        for m in range(micro):
            t_buf[m * pair:(m + 1) * pair, k * 128:(k + 1) * 128] = spread[:, m * 128:(m + 1) * 128]
        if k % 2 or k == TAPS - 1:
            low = k - k % 2 if k < TAPS - 1 else k
            block = jnp.dot(h_t, t_buf[:, low * 128:(k + 1) * 128], preferred_element_type=F32).astype(BF)
            for j in range(low, k + 1):
                out_ref[j * C:(j + 1) * C, :] = block[:, (j - low) * 128:(j - low + 1) * 128]
    out_ref[TAPS * C:, :] = jnp.zeros((out_ref.shape[0] - TAPS * C, 128), BF)


def sum_kernel(x_ref, out_ref):
    total = jnp.sum(x_ref[...].astype(F32), axis=0).astype(BF)
    out_ref[...] = jnp.broadcast_to(total[None], out_ref.shape)


def join_kernel(core_ref, mine, other, out_ref):
    for c in range(2):
        @pl.when(core_ref[0] == c)
        def _(c=c):
            rows = out_ref.shape[0]
            out_ref[:, c * 128:(c + 1) * 128] = mine[:rows]
            out_ref[:, (1 - c) * 128:(2 - c) * 128] = other[:rows]


VMEM = pl.BlockSpec(memory_space=pltpu.VMEM)
SMEM = pl.BlockSpec(memory_space=pltpu.SMEM)
ANY = pl.BlockSpec(memory_space=pl.ANY)
INTERPRET = False


def call(kernel, out_shape, in_specs, scratch=(), flops=0, nbytes=0, aliases=None):
    many = isinstance(out_shape, (tuple, list))
    return pl.pallas_call(
        kernel,
        out_shape=out_shape,
        in_specs=in_specs,
        out_specs=[VMEM] * len(out_shape) if many else VMEM,
        scratch_shapes=list(scratch),
        interpret=INTERPRET,
        input_output_aliases=aliases or {},
        cost_estimate=pl.CostEstimate(flops=flops, bytes_accessed=nbytes, transcendentals=0),
        compiler_params=pltpu.CompilerParams(vmem_limit_bytes=28 << 20),
    )


def prep_call(*operands):
    tiles, hot = FWD_TILES[0][1], (TAPS - 1) * TILE
    return call(
        prep_kernel,
        [
            jax.ShapeDtypeStruct((ROWS, C), BF),
            jax.ShapeDtypeStruct((ROWS, C), BF),
            jax.ShapeDtypeStruct((tiles, hot, 2 * TILE), BF),
            jax.ShapeDtypeStruct((BWD_TILES[3][1], hot, 2 * TILE), BF),
            jax.ShapeDtypeStruct((tiles * TILE, TAPS * C), BF),
            jax.ShapeDtypeStruct((TAPS - 1, 2 * PIX, 2 * PROWS), BF),
            jax.ShapeDtypeStruct((LEVELS, TAPS * C, C), BF),
        ],
        [SMEM] + [VMEM] * 7 + [ANY] * 2,
        [pltpu.VMEM((ROWS, 128), F32), pltpu.SemaphoreType.DMA((2,))],
        flops=10**9, nbytes=12 * 10**6,
    )(*operands)


def stack_call(*operands):
    tiles = FWD_TILES[0][1]
    return call(
        stack_kernel,
        [jax.ShapeDtypeStruct((LEVELS, MSG, C), BF), jax.ShapeDtypeStruct((LEVELS, TAPS * C, C), BF)],
        [SMEM] + [VMEM] * 6 + [ANY] * 3,
        [
            pltpu.VMEM((LEVELS - 1, ROWS, C), BF),
            pltpu.VMEM((tiles * TILE, TAPS * C), BF),
            pltpu.VMEM((LEVELS, tiles * TILE, C), F32),
            pltpu.VMEM((ROWS, C), BF),
            pltpu.VMEM((ROWS, C), BF),
            pltpu.SemaphoreType.DMA((3,)),
        ],
        flops=5 * 10**9, nbytes=10 * 10**6, aliases={6: 1},
    )(*operands)


def shift(axis_size, by):
    return [(i, (i + by) % axis_size) for i in range(axis_size)]


def step(maps, upstream, weights, neighbours):
    micro = maps.shape[0]
    section = lax.axis_index("section")
    core = lax.axis_index("core")
    patches = lax.axis_size("py") * lax.axis_size("core")
    patch = lax.axis_index("py") * lax.axis_size("core") + core
    cores = jnp.stack([core, section, patch]).astype(jnp.int32)

    sections = lax.axis_size("section")
    ways = [(2 * i + c, 2 * ((i + (1, -1)[c]) % sections) + c) for i in range(sections) for c in range(2)]
    near = lax.ppermute(weights[0], ("section", "core"), ways)
    half = lax.dynamic_slice_in_dim(near, core * HALF, HALF)
    far = lax.ppermute(half, ("section", "core"), ways)
    near_other = lax.ppermute(near, "core", shift(2, 1))
    far_other = lax.ppermute(far, "core", shift(2, 1))

    own, to2a, to2b, to3a, to3b = pack_call(cores, maps, upstream, neighbours)
    send = functools.partial(lax.ppermute, axis_name=("py", "core"))
    sends = []
    for block, by in ((to2b, -2), (own, -1), (own, 1), (to2a, 2), (to3b, -3), (to3a, 3)):
        sends.append(send(block, perm=shift(patches, by)))
    m2b, m1b, m1a, m2a, m3b, m3a = sends
    h0, g_top, s_hot, st_hot, gat0, hot, w_all = prep_call(
        cores, m3a, m2a, m1a, own, m1b, m2b, m3b, weights[0], near)
    out, _ = stack_call(cores, h0, g_top, s_hot, st_hot, gat0, w_all, near_other, far, far_other)

    mine = lax.all_to_all(out, "section", 0, 0, tiled=True)
    other = lax.ppermute(mine[:, :HROWS + PROWS], "core", shift(2, 1))
    chips = lax.axis_size("dp") * lax.axis_size("py")
    rows = (TAPS + 1) * C
    part, gin = call(
        grad_kernel,
        [jax.ShapeDtypeStruct((rows, 128), BF), jax.ShapeDtypeStruct((micro, PIX, C), BF)],
        [SMEM] + [VMEM] * 3,
        [
            pltpu.VMEM((2 * PROWS, micro * 128), BF),
            pltpu.VMEM((micro * 2 * PIX, C), BF),
            pltpu.VMEM((micro * 2 * PIX, TAPS * 128), BF),
        ],
        flops=10**9, nbytes=2 * 10**6,
    )(cores, mine, other, hot)
    pieces = lax.all_to_all(part.reshape((chips, rows // chips, 128)), ("dp", "py"), 0, 0, tiled=True)
    total = call(
        sum_kernel, jax.ShapeDtypeStruct(pieces.shape, BF), [VMEM], nbytes=10**6,
    )(pieces)
    full = lax.all_to_all(total, ("dp", "py"), 0, 0, tiled=True).reshape((rows, 128))
    swapped = lax.ppermute(full, "core", shift(2, 1))
    summed = call(
        join_kernel, jax.ShapeDtypeStruct((TAPS * C, C), BF), [SMEM, VMEM, VMEM], nbytes=2 * 10**6,
    )(cores, full, swapped)
    return (gin[None, :, None], summed[None])


def solution(mesh):
    size = dict(mesh.shape)
    grid = (size["dp"], size["section"], size["patch"] // 2, 2)
    fine = Mesh(mesh.devices.reshape(grid), ("dp", "section", "py", "core"))
    patch = ("py", "core")
    in_specs = (
        P(None, "dp", patch, None),
        P(None, "dp", patch, None),
        P("section", None, None),
        P(None, patch),
    )
    out_specs = (P("section", None, "dp", patch, None), P("section", None, None))
    return jax.shard_map(step, mesh=fine, in_specs=in_specs, out_specs=out_specs, check_vma=False)
```

```python
import functools

import jax
import jax.numpy as jnp
from jax import lax
from jax.experimental import pallas as pl
from jax.experimental.pallas import tpu as pltpu
from jax.sharding import Mesh
from jax.sharding import PartitionSpec as P


HALO = 32
TAPS = 9
C = 256
PIX = 96
LEVELS = 4
REACH = 2 * LEVELS * HALO
TILE = 64
PAD = 32
WIN = PIX + 2 * REACH
ROWS = WIN + 2 * PAD
HALF = TAPS * C // 2
BF = jnp.bfloat16
F32 = jnp.float32
NT = (((1,), (1,)), ((), ()))

FWD_ROWS = ((32, 576), (64, 544), (96, 512), (128, 480))
FWD_TILES = ((0, 9), (1, 9), (1, 8), (2, 8))
PRE_ROWS = ((224, 384), (192, 416), (160, 448), (128, 480))
BWD_ROWS = ((256, 352), (224, 384), (192, 416), (160, 448))
BWD_TILES = ((4, 6), (3, 6), (3, 7), (2, 7))
EDGE = 2 * HALO
OFF = 16
OWN = REACH
HROWS, PROWS, GROWS = PIX, PIX + HALO, PIX
FOLD = PROWS // 2
AT_H, AT_PRE, AT_G = FOLD, FOLD + HROWS, 2 * FOLD + HROWS
MSG = AT_G + GROWS


def expand(gat, t, src, hot):
    rows = jnp.dot(hot, src, preferred_element_type=F32).astype(BF)
    dst = pl.ds(pl.multiple_of(t * TILE, TILE), TILE)
    gat[dst, :C] = src[PAD:PAD + TILE]
    for k in range(1, TAPS):
        gat[dst, k * C:(k + 1) * C] = rows[(k - 1) * TILE:k * TILE]


def expand_all(gat, first, last, src_ref, hot_ref, group):
    def one(t):
        expand(gat, t, src_ref[pl.ds(pl.multiple_of(t * TILE, TILE), 2 * TILE), :], hot_ref[t])

    def some(i, carry):
        for j in range(group):
            one(first + i * group + j)
        return carry

    whole = (last - first) // group
    if whole:
        lax.fori_loop(0, whole, some, 0)
    for t in range(first + whole * group, last):
        one(t)


def pack_kernel(npix, ids_ref, maps, upstream, neighbours, own, to2a, to2b, to3a, to3b, off_buf):
    start, top = maps[0, 0], upstream[0, 0]
    place = ids_ref[2] * PIX + lax.broadcasted_iota(jnp.int32, (TAPS, PIX), 1)
    offsets = neighbours[...] - place + HALO
    offsets = jnp.where(offsets < 0, offsets + npix, offsets)
    offsets = jnp.where(offsets >= npix, offsets - npix, offsets) - HALO
    off_buf[...] = jnp.zeros_like(off_buf)
    off_buf[:TAPS, :PIX] = offsets.astype(F32)
    tail = off_buf[...].astype(BF)
    for ref, rows in ((own, (start, top)), (to2a, (start, top[PIX - HALO:])), (to2b, (start, top[:HALO])),
                      (to3a, (start[PIX - EDGE:],)), (to3b, (start[:EDGE],))):
        at = 0
        for value in (*rows, tail):
            ref[at:at + value.shape[0], :] = value
            at += value.shape[0]


def pack_call(ids, maps, upstream, neighbours):
    npix = PIX * lax.axis_size("py") * lax.axis_size("core")
    mine = pl.BlockSpec((1, 1, PIX, C), lambda i, ids: (ids[1], 0, 0, 0))
    rows = [2 * PIX + OFF, PIX + HALO + OFF, PIX + HALO + OFF, EDGE + OFF, EDGE + OFF]
    return pl.pallas_call(
        functools.partial(pack_kernel, npix),
        grid_spec=pltpu.PrefetchScalarGridSpec(
            num_scalar_prefetch=1,
            grid=(1,),
            in_specs=[mine, mine, pl.BlockSpec((TAPS, PIX), lambda i, ids: (0, 0))],
            out_specs=[pl.BlockSpec((n, C), lambda i, ids: (0, 0)) for n in rows],
            scratch_shapes=[pltpu.VMEM((OFF, C), F32)],
        ),
        out_shape=[jax.ShapeDtypeStruct((n, C), BF) for n in rows],
        interpret=INTERPRET,
        cost_estimate=pl.CostEstimate(flops=0, bytes_accessed=10**6, transcendentals=0),
    )(ids, maps, upstream, neighbours)


def prep_kernel(ids_ref, m3a, m2a, m1a, own, m1b, m2b, m3b, w_own, near_mine, near_other,
                h_ref, g_ref, s_ref, st_ref, gat_ref, pair_ref, w_ref, off_buf, sems):
    core, section = ids_ref[0], ids_ref[1]
    left, right = lax.rem(section + 3, LEVELS), lax.rem(section + 1, LEVELS)
    copies = []
    for n, (src, level) in enumerate((
        (w_own, section),
        (near_mine, jnp.where(core == 0, left, right)),
        (near_other, jnp.where(core == 0, right, left)),
    )):
        copies.append(pltpu.make_async_copy(src, w_ref.at[level], sems.at[n]))
        copies[-1].start()
    h_ref[:PAD, :] = jnp.zeros((PAD, C), BF)
    h_ref[ROWS - PAD:, :] = jnp.zeros((PAD, C), BF)
    g_ref[...] = jnp.zeros_like(g_ref)
    off_buf[:PAD, :] = jnp.zeros((PAD, 128), F32)
    off_buf[ROWS - PAD:, :] = jnp.zeros((PAD, 128), F32)
    at = PAD
    shapes = ((EDGE, PIX - EDGE, 0, 0), (PIX, 0, HALO, PIX - HALO), (PIX, 0, PIX, 0), (PIX, 0, PIX, 0),
              (PIX, 0, PIX, 0), (PIX, 0, HALO, 0), (EDGE, 0, 0, 0))
    for piece, (n, first, n_top, first_top) in zip((m3a, m2a, m1a, own, m1b, m2b, m3b), shapes):
        h_ref[at:at + n, :] = piece[:n, :]
        if n_top:
            place = at + first_top
            g_ref[place:place + n_top, :] = piece[n:n + n_top, :]
        off_t = jnp.transpose(piece[n + n_top:, :128].astype(F32))
        off_buf[at:at + n, :OFF] = off_t[first:first + n]
        at += n

    rel = (lax.broadcasted_iota(jnp.int32, (TILE, 128), 1)
           - lax.broadcasted_iota(jnp.int32, (TILE, 128), 0) - HALO).astype(F32)

    def build_s(t, carry):
        d = off_buf[pl.ds(pl.multiple_of(t * TILE + PAD, PAD), TILE), :]
        for k in range(1, TAPS):
            hit = rel == d[:, k:k + 1]
            s_ref[t, (k - 1) * TILE:k * TILE, :] = jnp.where(hit, 1.0, 0.0).astype(BF)
        return carry

    lax.fori_loop(0, FWD_TILES[0][1], build_s, 0)

    def build_st(t, carry):
        d = jnp.transpose(off_buf[pl.ds(pl.multiple_of(t * TILE, TILE), 128), :])
        for k in range(1, TAPS):
            hit = -rel == d[k:k + 1, :]
            st_ref[t, (k - 1) * TILE:k * TILE, :] = jnp.where(hit, 1.0, 0.0).astype(BF)
        return carry

    lax.fori_loop(BWD_TILES[3][0], BWD_TILES[3][1], build_st, 0)
    expand_all(gat_ref, *FWD_TILES[0], h_ref, s_ref, 3)

    start = pl.multiple_of(PAD + OWN - HALO - PIX * core, HALO)
    offt = jnp.transpose(off_buf[pl.ds(start, 2 * PROWS), :])
    apart = (lax.broadcasted_iota(jnp.int32, (2 * PIX, 2 * PROWS), 0)
             - lax.broadcasted_iota(jnp.int32, (2 * PIX, 2 * PROWS), 1) + HALO).astype(F32)
    for k in range(1, TAPS):
        pair_ref[k - 1] = jnp.where(apart == offt[k:k + 1, :], 1.0, 0.0).astype(BF)
    for copy in copies:
        copy.wait()


def stack_kernel(ids_ref, h0, g_top, s_buf, st_buf, gat0, w_in, far_mine, far_other,
                 out_ref, w_buf, h_buf, gat, der, pre_buf, g_buf, sems):
    core, section = ids_ref[0], ids_ref[1]
    del w_in
    far = w_buf.at[lax.rem(section + 2, LEVELS)]
    copies = []
    for n, (src, dst) in enumerate((
        (far_mine, far.at[pl.ds(pl.multiple_of(core * HALF, HALF), HALF), :]),
        (far_other, far.at[pl.ds(pl.multiple_of((1 - core) * HALF, HALF), HALF), :]),
    )):
        copies.append(pltpu.make_async_copy(src, dst, sems.at[n]))
        copies[-1].start()
    h_buf[...] = jnp.zeros_like(h_buf)
    pre_buf[...] = jnp.zeros_like(pre_buf)
    g_buf[...] = g_top[...]
    for copy in copies:
        copy.wait()

    for level in range(LEVELS):
        first, last = FWD_TILES[level]

        src = h0 if level == 0 else h_buf.at[level - 1]
        rows = gat0 if level == 0 else gat
        if level:
            expand_all(gat, first, last, src, s_buf, 3)
        lo, hi = FWD_ROWS[level]
        act = jnp.dot(rows[lo:hi, :], w_buf[level], preferred_element_type=F32)
        squash = jnp.tanh(act)
        der[level, lo:hi, :] = 1.0 - squash * squash
        if level + 1 < LEVELS:
            h_buf[level, PAD + lo:PAD + hi, :] = (src[PAD + lo:PAD + hi, :].astype(F32) + squash).astype(BF)
        out_ref[level, AT_H:AT_PRE, :] = src[PAD + OWN:PAD + OWN + PIX, :]

    for level in range(LEVELS - 1, -1, -1):
        lo, hi = PRE_ROWS[level]
        pre_buf[PAD + lo:PAD + hi, :] = (
            g_buf[PAD + lo:PAD + hi, :].astype(F32) * der[level, lo:hi, :]).astype(BF)
        first, last = BWD_TILES[level]

        expand_all(gat, first, last, pre_buf, st_buf, 3)
        lo, hi = BWD_ROWS[level]
        total = g_buf[PAD + lo:PAD + hi, :].astype(F32)
        for k in range(TAPS):
            total = total + lax.dot_general(gat[lo:hi, k * C:(k + 1) * C],
                                            w_buf[level, k * C:(k + 1) * C, :], NT,
                                            preferred_element_type=F32)
        g_buf[PAD + lo:PAD + hi, :] = total.astype(BF)
        start = pl.multiple_of(PAD + OWN - HALO + HALO * core, HALO)
        for at, half in ((0, 1 - core), (AT_PRE, core)):
            part = pre_buf[pl.ds(start, PROWS), pl.ds(pl.multiple_of(half * 128, 128), 128)]
            out_ref[level, at:at + FOLD, :128] = part[:FOLD]
            out_ref[level, at:at + FOLD, 128:] = part[FOLD:]
        out_ref[level, AT_G:, :] = g_buf[PAD + OWN:PAD + OWN + PIX, :]


def grad_kernel(core_ref, mine, other, hot, out_ref, gin_ref, p_buf, h_buf, t_buf):
    core = core_ref[0]
    micro = mine.shape[0]
    pair = 2 * PIX
    gin_ref[...] = mine[:, AT_G:, :]
    for c in range(2):
        @pl.when(core == c)
        def _(c=c):
            both = ((mine, AT_PRE), (other, 0))
            for m in range(micro):
                for n, (ref, at) in enumerate(both if c == 0 else both[::-1]):
                    for side in range(2):
                        to = n * PROWS + side * FOLD
                        p_buf[to:to + FOLD, m * 128:(m + 1) * 128] = (
                            ref[m, at:at + FOLD, side * 128:(side + 1) * 128])
                    h_buf[m * pair + n * PIX:m * pair + (n + 1) * PIX, :] = ref[m, AT_H:AT_PRE, :]
    h_t = jnp.transpose(h_buf[...].astype(F32)).astype(BF)
    pre = p_buf[...]
    for k in range(TAPS):
        if k == 0:
            spread = pre[HALO:HALO + pair]
        else:
            spread = jnp.dot(hot[k - 1], pre, preferred_element_type=F32).astype(BF)
        for m in range(micro):
            t_buf[m * pair:(m + 1) * pair, k * 128:(k + 1) * 128] = spread[:, m * 128:(m + 1) * 128]
        if k % 2 or k == TAPS - 1:
            low = k - k % 2 if k < TAPS - 1 else k
            block = jnp.dot(h_t, t_buf[:, low * 128:(k + 1) * 128], preferred_element_type=F32).astype(BF)
            for j in range(low, k + 1):
                out_ref[j * C:(j + 1) * C, :] = block[:, (j - low) * 128:(j - low + 1) * 128]


def sum_kernel(size, x_ref, out_ref):
    pairs = x_ref.shape[0] // (2 * size)
    total = x_ref[:2 * size, :].astype(F32)
    for n in range(1, pairs):
        total = total + x_ref[2 * size * n:2 * size * (n + 1), :].astype(F32)
    total = total[:size] + total[size:]
    total = jnp.concatenate([total, total]).astype(BF)
    for n in range(pairs):
        out_ref[2 * size * n:2 * size * (n + 1), :] = total


def place_kernel(side, core_ref, half, *refs):
    out_ref, sem = refs[-2:]
    column = pl.multiple_of(jnp.abs(core_ref[0] - side) * 128, 128)
    copy = pltpu.make_async_copy(half, out_ref.at[:, pl.ds(column, 128)], sem)
    copy.start()
    copy.wait()


VMEM = pl.BlockSpec(memory_space=pltpu.VMEM)
SMEM = pl.BlockSpec(memory_space=pltpu.SMEM)
ANY = pl.BlockSpec(memory_space=pl.ANY)
INTERPRET = False


def call(kernel, out_shape, in_specs, scratch=(), flops=0, nbytes=0, aliases=None, out_spec=None):
    many = isinstance(out_shape, (tuple, list))
    return pl.pallas_call(
        kernel,
        out_shape=out_shape,
        in_specs=in_specs,
        out_specs=[VMEM] * len(out_shape) if many else out_spec or VMEM,
        scratch_shapes=list(scratch),
        interpret=INTERPRET,
        input_output_aliases=aliases or {},
        cost_estimate=pl.CostEstimate(flops=flops, bytes_accessed=nbytes, transcendentals=0),
        compiler_params=pltpu.CompilerParams(vmem_limit_bytes=28 << 20),
    )


def prep_call(*operands):
    tiles, hot = FWD_TILES[0][1], (TAPS - 1) * TILE
    return call(
        prep_kernel,
        [
            jax.ShapeDtypeStruct((ROWS, C), BF),
            jax.ShapeDtypeStruct((ROWS, C), BF),
            jax.ShapeDtypeStruct((tiles, hot, 2 * TILE), BF),
            jax.ShapeDtypeStruct((BWD_TILES[3][1], hot, 2 * TILE), BF),
            jax.ShapeDtypeStruct((tiles * TILE, TAPS * C), BF),
            jax.ShapeDtypeStruct((TAPS - 1, 2 * PIX, 2 * PROWS), BF),
            jax.ShapeDtypeStruct((LEVELS, TAPS * C, C), BF),
        ],
        [SMEM] + [VMEM] * 7 + [ANY] * 3,
        [pltpu.VMEM((ROWS, 128), F32), pltpu.SemaphoreType.DMA((3,))],
        flops=10**9, nbytes=12 * 10**6,
    )(*operands)


def stack_call(*operands):
    tiles = FWD_TILES[0][1]
    return call(
        stack_kernel,
        [jax.ShapeDtypeStruct((LEVELS, MSG, C), BF), jax.ShapeDtypeStruct((LEVELS, TAPS * C, C), BF)],
        [SMEM] + [VMEM] * 6 + [ANY] * 2,
        [
            pltpu.VMEM((LEVELS - 1, ROWS, C), BF),
            pltpu.VMEM((tiles * TILE, TAPS * C), BF),
            pltpu.VMEM((LEVELS, tiles * TILE, C), F32),
            pltpu.VMEM((ROWS, C), BF),
            pltpu.VMEM((ROWS, C), BF),
            pltpu.SemaphoreType.DMA((2,)),
        ],
        flops=5 * 10**9, nbytes=10 * 10**6, aliases={6: 1},
    )(*operands)


def shift(axis_size, by):
    return [(i, (i + by) % axis_size) for i in range(axis_size)]


def step(maps, upstream, weights, neighbours):
    micro = maps.shape[0]
    section = lax.axis_index("section")
    core = lax.axis_index("core")
    patches = lax.axis_size("py") * lax.axis_size("core")
    patch = lax.axis_index("py") * lax.axis_size("core") + core
    cores = jnp.stack([core, section, patch]).astype(jnp.int32)

    sections = lax.axis_size("section")
    ways = [(2 * i + c, 2 * ((i + (1, -1)[c]) % sections) + c) for i in range(sections) for c in range(2)]
    near = lax.ppermute(weights[0], ("section", "core"), ways)
    half = lax.dynamic_slice_in_dim(near, core * HALF, HALF)
    far = lax.ppermute(half, ("section", "core"), ways)
    near_other = lax.ppermute(near, "core", shift(2, 1))
    far_other = lax.ppermute(far, "core", shift(2, 1))

    own, to2a, to2b, to3a, to3b = pack_call(cores, maps, upstream, neighbours)
    send = functools.partial(lax.ppermute, axis_name=("py", "core"))
    sends = []
    for block, by in ((to2b, -2), (own, -1), (own, 1), (to2a, 2), (to3b, -3), (to3a, 3)):
        sends.append(send(block, perm=shift(patches, by)))
    m2b, m1b, m1a, m2a, m3b, m3a = sends
    h0, g_top, s_hot, st_hot, gat0, hot, w_all = prep_call(
        cores, m3a, m2a, m1a, own, m1b, m2b, m3b, weights[0], near, near_other)
    out, _ = stack_call(cores, h0, g_top, s_hot, st_hot, gat0, w_all, far, far_other)

    mine = lax.all_to_all(out, "section", 0, 0, tiled=True)
    other = lax.ppermute(mine[:, :AT_PRE], "core", shift(2, 1))
    chips = lax.axis_size("dp") * lax.axis_size("py")
    rows = TAPS * C
    blocks = (chips, rows // chips // 4, 4, 128)
    part, gin = call(
        grad_kernel,
        [jax.ShapeDtypeStruct((rows, 128), BF), jax.ShapeDtypeStruct((micro, PIX, C), BF)],
        [SMEM] + [VMEM] * 3,
        [
            pltpu.VMEM((2 * PROWS, micro * 128), BF),
            pltpu.VMEM((micro * 2 * PIX, C), BF),
            pltpu.VMEM((micro * 2 * PIX, TAPS * 128), BF),
        ],
        flops=10**9, nbytes=2 * 10**6,
    )(cores, mine, other, hot)
    pieces = lax.all_to_all(part.reshape(blocks), ("dp", "py"), 0, 0, tiled=True)
    total = call(
        functools.partial(sum_kernel, rows // chips), jax.ShapeDtypeStruct((rows, 128), BF), [VMEM], nbytes=10**6,
    )(pieces.reshape((rows, 128)))
    full = lax.all_to_all(total.reshape(blocks), ("dp", "py"), 0, 0, tiled=True).reshape((rows, 128))
    swapped = lax.ppermute(full, "core", shift(2, 1))
    out_shape = jax.ShapeDtypeStruct((rows, C), BF)
    sem = [pltpu.SemaphoreType.DMA]
    half_done = call(functools.partial(place_kernel, 0), out_shape, [SMEM, ANY], sem, nbytes=10**6, out_spec=ANY)(
        cores, full)
    summed = call(functools.partial(place_kernel, 1), out_shape, [SMEM, ANY, ANY], sem, nbytes=10**6, aliases={2: 0},
                  out_spec=ANY)(cores, swapped, half_done)
    return (gin[None, :, None], summed[None])


def solution(mesh):
    size = dict(mesh.shape)
    grid = (size["dp"], size["section"], size["patch"] // 2, 2)
    fine = Mesh(mesh.devices.reshape(grid), ("dp", "section", "py", "core"))
    patch = ("py", "core")
    in_specs = (
        P(None, "dp", patch, None),
        P(None, "dp", patch, None),
        P("section", None, None),
        P(None, patch),
    )
    out_specs = (P("section", None, "dp", patch, None), P("section", None, None))
    return jax.shard_map(step, mesh=fine, in_specs=in_specs, out_specs=out_specs, check_vma=False)
```

```python
import functools

import jax
import jax.numpy as jnp
from jax import lax
from jax.experimental import pallas as pl
from jax.experimental.pallas import tpu as pltpu
from jax.sharding import Mesh
from jax.sharding import PartitionSpec as P


HALO = 32
TAPS = 9
C = 256
PIX = 96
LEVELS = 4
REACH = 2 * LEVELS * HALO
TILE = 64
PAD = 32
WIN = PIX + 2 * REACH
ROWS = WIN + 2 * PAD
HALF = TAPS * C // 2
BF = jnp.bfloat16
F32 = jnp.float32
NT = (((1,), (1,)), ((), ()))

FWD_ROWS = ((32, 576), (64, 544), (96, 512), (128, 480))
FWD_TILES = ((0, 9), (1, 9), (1, 8), (2, 8))
PRE_ROWS = ((224, 384), (192, 416), (160, 448), (128, 480))
BWD_ROWS = ((256, 352), (224, 384), (192, 416), (160, 448))
BWD_TILES = ((4, 6), (3, 6), (3, 7), (2, 7))
EDGE = 2 * HALO
OFF = 16
OWN = REACH
HROWS, PROWS, GROWS = PIX, PIX + HALO, PIX
FOLD = PROWS // 2
AT_H, AT_PRE, AT_G = FOLD, FOLD + HROWS, 2 * FOLD + HROWS
MSG = AT_G + GROWS


def expand(gat, t, src, hot):
    rows = jnp.dot(hot, src, preferred_element_type=F32).astype(BF)
    dst = pl.ds(pl.multiple_of(t * TILE, TILE), TILE)
    gat[dst, :C] = src[PAD:PAD + TILE]
    for k in range(1, TAPS):
        gat[dst, k * C:(k + 1) * C] = rows[(k - 1) * TILE:k * TILE]


def expand_all(gat, first, last, src_ref, hot_ref, group):
    def one(t):
        expand(gat, t, src_ref[pl.ds(pl.multiple_of(t * TILE, TILE), 2 * TILE), :], hot_ref[t])

    def some(i, carry):
        for j in range(group):
            one(first + i * group + j)
        return carry

    whole = (last - first) // group
    if whole:
        lax.fori_loop(0, whole, some, 0)
    for t in range(first + whole * group, last):
        one(t)


def pack_kernel(npix, ids_ref, maps, upstream, neighbours, own, to2a, to2b, to3a, to3b, off_buf):
    start, top = maps[0, 0], upstream[0, 0]
    place = ids_ref[2] * PIX + lax.broadcasted_iota(jnp.int32, (TAPS, PIX), 1)
    offsets = neighbours[...] - place + HALO
    offsets = jnp.where(offsets < 0, offsets + npix, offsets)
    offsets = jnp.where(offsets >= npix, offsets - npix, offsets) - HALO
    off_buf[...] = jnp.zeros_like(off_buf)
    off_buf[:TAPS, :PIX] = offsets.astype(F32)
    tail = off_buf[...].astype(BF)
    for ref, rows in ((own, (start, top)), (to2a, (start, top[PIX - HALO:])), (to2b, (start, top[:HALO])),
                      (to3a, (start[PIX - EDGE:],)), (to3b, (start[:EDGE],))):
        at = 0
        for value in (*rows, tail):
            ref[at:at + value.shape[0], :] = value
            at += value.shape[0]


def pack_call(ids, maps, upstream, neighbours):
    npix = PIX * lax.axis_size("py") * lax.axis_size("core")
    mine = pl.BlockSpec((1, 1, PIX, C), lambda i, ids: (ids[1], 0, 0, 0))
    rows = [2 * PIX + OFF, PIX + HALO + OFF, PIX + HALO + OFF, EDGE + OFF, EDGE + OFF]
    return pl.pallas_call(
        functools.partial(pack_kernel, npix),
        grid_spec=pltpu.PrefetchScalarGridSpec(
            num_scalar_prefetch=1,
            grid=(1,),
            in_specs=[mine, mine, pl.BlockSpec((TAPS, PIX), lambda i, ids: (0, 0))],
            out_specs=[pl.BlockSpec((n, C), lambda i, ids: (0, 0)) for n in rows],
            scratch_shapes=[pltpu.VMEM((OFF, C), F32)],
        ),
        out_shape=[jax.ShapeDtypeStruct((n, C), BF) for n in rows],
        interpret=INTERPRET,
        cost_estimate=pl.CostEstimate(flops=0, bytes_accessed=10**6, transcendentals=0),
    )(ids, maps, upstream, neighbours)


def prep_kernel(ids_ref, m3a, m2a, m1a, own, m1b, m2b, m3b, w_own, near_mine,
                h_ref, g_ref, s_ref, st_ref, gat_ref, pair_ref, w_ref, off_buf, sems):
    core, section = ids_ref[0], ids_ref[1]
    left, right = lax.rem(section + 3, LEVELS), lax.rem(section + 1, LEVELS)
    copies = []
    for n, (src, level) in enumerate((
        (w_own, section),
        (near_mine, jnp.where(core == 0, left, right)),
    )):
        copies.append(pltpu.make_async_copy(src, w_ref.at[level], sems.at[n]))
        copies[-1].start()
    h_ref[:PAD, :] = jnp.zeros((PAD, C), BF)
    h_ref[ROWS - PAD:, :] = jnp.zeros((PAD, C), BF)
    g_ref[...] = jnp.zeros_like(g_ref)
    off_buf[:PAD, :] = jnp.zeros((PAD, 128), F32)
    off_buf[ROWS - PAD:, :] = jnp.zeros((PAD, 128), F32)
    at = PAD
    shapes = ((EDGE, PIX - EDGE, 0, 0), (PIX, 0, HALO, PIX - HALO), (PIX, 0, PIX, 0), (PIX, 0, PIX, 0),
              (PIX, 0, PIX, 0), (PIX, 0, HALO, 0), (EDGE, 0, 0, 0))
    for piece, (n, first, n_top, first_top) in zip((m3a, m2a, m1a, own, m1b, m2b, m3b), shapes):
        h_ref[at:at + n, :] = piece[:n, :]
        if n_top:
            place = at + first_top
            g_ref[place:place + n_top, :] = piece[n:n + n_top, :]
        off_t = jnp.transpose(piece[n + n_top:, :128].astype(F32))
        off_buf[at:at + n, :OFF] = off_t[first:first + n]
        at += n

    rel = (lax.broadcasted_iota(jnp.int32, (TILE, 128), 1)
           - lax.broadcasted_iota(jnp.int32, (TILE, 128), 0) - HALO).astype(F32)

    def build_s(t, carry):
        d = off_buf[pl.ds(pl.multiple_of(t * TILE + PAD, PAD), TILE), :]
        for k in range(1, TAPS):
            hit = rel == d[:, k:k + 1]
            s_ref[t, (k - 1) * TILE:k * TILE, :] = jnp.where(hit, 1.0, 0.0).astype(BF)
        return carry

    lax.fori_loop(0, FWD_TILES[0][1], build_s, 0)

    def build_st(t, carry):
        d = jnp.transpose(off_buf[pl.ds(pl.multiple_of(t * TILE, TILE), 128), :])
        for k in range(1, TAPS):
            hit = -rel == d[k:k + 1, :]
            st_ref[t, (k - 1) * TILE:k * TILE, :] = jnp.where(hit, 1.0, 0.0).astype(BF)
        return carry

    lax.fori_loop(BWD_TILES[3][0], BWD_TILES[3][1], build_st, 0)
    expand_all(gat_ref, *FWD_TILES[0], h_ref, s_ref, 3)

    start = pl.multiple_of(PAD + OWN - HALO - PIX * core, HALO)
    offt = jnp.transpose(off_buf[pl.ds(start, 2 * PROWS), :])
    apart = (lax.broadcasted_iota(jnp.int32, (2 * PIX, 2 * PROWS), 0)
             - lax.broadcasted_iota(jnp.int32, (2 * PIX, 2 * PROWS), 1) + HALO).astype(F32)
    for k in range(1, TAPS):
        pair_ref[k - 1] = jnp.where(apart == offt[k:k + 1, :], 1.0, 0.0).astype(BF)
    for copy in copies:
        copy.wait()


def stack_kernel(ids_ref, h0, g_top, s_buf, st_buf, gat0, w_in, near_other, far_mine, far_other,
                 out_ref, w_buf, h_buf, gat, der, pre_buf, g_buf, sems):
    core, section = ids_ref[0], ids_ref[1]
    del w_in
    far = w_buf.at[lax.rem(section + 2, LEVELS)]
    copies = []
    for n, (src, dst) in enumerate((
        (near_other, w_buf.at[lax.rem(section + 1 + 2 * core, LEVELS)]),
        (far_mine, far.at[pl.ds(pl.multiple_of(core * HALF, HALF), HALF), :]),
        (far_other, far.at[pl.ds(pl.multiple_of((1 - core) * HALF, HALF), HALF), :]),
    )):
        copies.append(pltpu.make_async_copy(src, dst, sems.at[n]))
        copies[-1].start()
    h_buf[...] = jnp.zeros_like(h_buf)
    pre_buf[...] = jnp.zeros_like(pre_buf)
    g_buf[...] = g_top[...]
    for copy in copies:
        copy.wait()

    for level in range(LEVELS):
        first, last = FWD_TILES[level]

        src = h0 if level == 0 else h_buf.at[level - 1]
        rows = gat0 if level == 0 else gat
        if level:
            expand_all(gat, first, last, src, s_buf, 3)
        lo, hi = FWD_ROWS[level]
        act = jnp.dot(rows[lo:hi, :], w_buf[level], preferred_element_type=F32)
        squash = jnp.tanh(act)
        der[level, lo:hi, :] = 1.0 - squash * squash
        if level + 1 < LEVELS:
            h_buf[level, PAD + lo:PAD + hi, :] = (src[PAD + lo:PAD + hi, :].astype(F32) + squash).astype(BF)
        out_ref[level, AT_H:AT_PRE, :] = src[PAD + OWN:PAD + OWN + PIX, :]

    for level in range(LEVELS - 1, -1, -1):
        lo, hi = PRE_ROWS[level]
        pre_buf[PAD + lo:PAD + hi, :] = (
            g_buf[PAD + lo:PAD + hi, :].astype(F32) * der[level, lo:hi, :]).astype(BF)
        first, last = BWD_TILES[level]

        expand_all(gat, first, last, pre_buf, st_buf, 3)
        lo, hi = BWD_ROWS[level]
        total = g_buf[PAD + lo:PAD + hi, :].astype(F32)
        for k in range(TAPS):
            total = total + lax.dot_general(gat[lo:hi, k * C:(k + 1) * C],
                                            w_buf[level, k * C:(k + 1) * C, :], NT,
                                            preferred_element_type=F32)
        g_buf[PAD + lo:PAD + hi, :] = total.astype(BF)
        start = pl.multiple_of(PAD + OWN - HALO + HALO * core, HALO)
        for at, half in ((0, 1 - core), (AT_PRE, core)):
            part = pre_buf[pl.ds(start, PROWS), pl.ds(pl.multiple_of(half * 128, 128), 128)]
            out_ref[level, at:at + FOLD, :128] = part[:FOLD]
            out_ref[level, at:at + FOLD, 128:] = part[FOLD:]
        out_ref[level, AT_G:, :] = g_buf[PAD + OWN:PAD + OWN + PIX, :]


def grad_kernel(core_ref, mine, other, hot, out_ref, gin_ref, p_buf, h_buf, t_buf):
    core = core_ref[0]
    micro = mine.shape[0]
    pair = 2 * PIX
    gin_ref[...] = mine[:, AT_G:, :]
    for c in range(2):
        @pl.when(core == c)
        def _(c=c):
            both = ((mine, AT_PRE), (other, 0))
            for m in range(micro):
                for n, (ref, at) in enumerate(both if c == 0 else both[::-1]):
                    for side in range(2):
                        to = n * PROWS + side * FOLD
                        p_buf[to:to + FOLD, m * 128:(m + 1) * 128] = (
                            ref[m, at:at + FOLD, side * 128:(side + 1) * 128])
                    h_buf[m * pair + n * PIX:m * pair + (n + 1) * PIX, :] = ref[m, AT_H:AT_PRE, :]
    h_t = jnp.transpose(h_buf[...].astype(F32)).astype(BF)
    pre = p_buf[...]
    for k in range(TAPS):
        if k == 0:
            spread = pre[HALO:HALO + pair]
        else:
            spread = jnp.dot(hot[k - 1], pre, preferred_element_type=F32).astype(BF)
        for m in range(micro):
            t_buf[m * pair:(m + 1) * pair, k * 128:(k + 1) * 128] = spread[:, m * 128:(m + 1) * 128]
        if k % 2 or k == TAPS - 1:
            low = k - k % 2 if k < TAPS - 1 else k
            block = jnp.dot(h_t, t_buf[:, low * 128:(k + 1) * 128], preferred_element_type=F32).astype(BF)
            for j in range(low, k + 1):
                out_ref[j * C:(j + 1) * C, :] = block[:, (j - low) * 128:(j - low + 1) * 128]


def sum_kernel(size, x_ref, out_ref):
    pairs = x_ref.shape[0] // (2 * size)
    total = x_ref[:2 * size, :].astype(F32)
    for n in range(1, pairs):
        total = total + x_ref[2 * size * n:2 * size * (n + 1), :].astype(F32)
    total = total[:size] + total[size:]
    total = jnp.concatenate([total, total]).astype(BF)
    for n in range(pairs):
        out_ref[2 * size * n:2 * size * (n + 1), :] = total


def place_kernel(side, core_ref, half, *refs):
    out_ref, sem = refs[-2:]
    column = pl.multiple_of(jnp.abs(core_ref[0] - side) * 128, 128)
    copy = pltpu.make_async_copy(half, out_ref.at[:, pl.ds(column, 128)], sem)
    copy.start()
    copy.wait()


VMEM = pl.BlockSpec(memory_space=pltpu.VMEM)
SMEM = pl.BlockSpec(memory_space=pltpu.SMEM)
ANY = pl.BlockSpec(memory_space=pl.ANY)
INTERPRET = False


def call(kernel, out_shape, in_specs, scratch=(), flops=0, nbytes=0, aliases=None, out_spec=None):
    many = isinstance(out_shape, (tuple, list))
    return pl.pallas_call(
        kernel,
        out_shape=out_shape,
        in_specs=in_specs,
        out_specs=[VMEM] * len(out_shape) if many else out_spec or VMEM,
        scratch_shapes=list(scratch),
        interpret=INTERPRET,
        input_output_aliases=aliases or {},
        cost_estimate=pl.CostEstimate(flops=flops, bytes_accessed=nbytes, transcendentals=0),
        compiler_params=pltpu.CompilerParams(vmem_limit_bytes=28 << 20),
    )


def prep_call(*operands):
    tiles, hot = FWD_TILES[0][1], (TAPS - 1) * TILE
    return call(
        prep_kernel,
        [
            jax.ShapeDtypeStruct((ROWS, C), BF),
            jax.ShapeDtypeStruct((ROWS, C), BF),
            jax.ShapeDtypeStruct((tiles, hot, 2 * TILE), BF),
            jax.ShapeDtypeStruct((BWD_TILES[3][1], hot, 2 * TILE), BF),
            jax.ShapeDtypeStruct((tiles * TILE, TAPS * C), BF),
            jax.ShapeDtypeStruct((TAPS - 1, 2 * PIX, 2 * PROWS), BF),
            jax.ShapeDtypeStruct((LEVELS, TAPS * C, C), BF),
        ],
        [SMEM] + [VMEM] * 7 + [ANY] * 2,
        [pltpu.VMEM((ROWS, 128), F32), pltpu.SemaphoreType.DMA((2,))],
        flops=10**9, nbytes=12 * 10**6,
    )(*operands)


def stack_call(*operands):
    tiles = FWD_TILES[0][1]
    return call(
        stack_kernel,
        [jax.ShapeDtypeStruct((LEVELS, MSG, C), BF), jax.ShapeDtypeStruct((LEVELS, TAPS * C, C), BF)],
        [SMEM] + [VMEM] * 6 + [ANY] * 3,
        [
            pltpu.VMEM((LEVELS - 1, ROWS, C), BF),
            pltpu.VMEM((tiles * TILE, TAPS * C), BF),
            pltpu.VMEM((LEVELS, tiles * TILE, C), F32),
            pltpu.VMEM((ROWS, C), BF),
            pltpu.VMEM((ROWS, C), BF),
            pltpu.SemaphoreType.DMA((3,)),
        ],
        flops=5 * 10**9, nbytes=10 * 10**6, aliases={6: 1},
    )(*operands)


def shift(axis_size, by):
    return [(i, (i + by) % axis_size) for i in range(axis_size)]


def step(maps, upstream, weights, neighbours):
    micro = maps.shape[0]
    section = lax.axis_index("section")
    core = lax.axis_index("core")
    patches = lax.axis_size("py") * lax.axis_size("core")
    patch = lax.axis_index("py") * lax.axis_size("core") + core
    cores = jnp.stack([core, section, patch]).astype(jnp.int32)

    sections = lax.axis_size("section")
    ways = [(2 * i + c, 2 * ((i + (1, -1)[c]) % sections) + c) for i in range(sections) for c in range(2)]
    near = lax.ppermute(weights[0], ("section", "core"), ways)
    half = lax.dynamic_slice_in_dim(near, core * HALF, HALF)
    far = lax.ppermute(half, ("section", "core"), ways)
    near_other = lax.ppermute(near, "core", shift(2, 1))
    far_other = lax.ppermute(far, "core", shift(2, 1))

    own, to2a, to2b, to3a, to3b = pack_call(cores, maps, upstream, neighbours)
    send = functools.partial(lax.ppermute, axis_name=("py", "core"))
    sends = []
    for block, by in ((to2b, -2), (own, -1), (own, 1), (to2a, 2), (to3b, -3), (to3a, 3)):
        sends.append(send(block, perm=shift(patches, by)))
    m2b, m1b, m1a, m2a, m3b, m3a = sends
    h0, g_top, s_hot, st_hot, gat0, hot, w_all = prep_call(
        cores, m3a, m2a, m1a, own, m1b, m2b, m3b, weights[0], near)
    out, _ = stack_call(cores, h0, g_top, s_hot, st_hot, gat0, w_all, near_other, far, far_other)

    mine = lax.all_to_all(out, "section", 0, 0, tiled=True)
    other = lax.ppermute(mine[:, :AT_PRE], "core", shift(2, 1))
    chips = lax.axis_size("dp") * lax.axis_size("py")
    rows = TAPS * C
    blocks = (chips, rows // chips // 4, 4, 128)
    part, gin = call(
        grad_kernel,
        [jax.ShapeDtypeStruct((rows, 128), BF), jax.ShapeDtypeStruct((micro, PIX, C), BF)],
        [SMEM] + [VMEM] * 3,
        [
            pltpu.VMEM((2 * PROWS, micro * 128), BF),
            pltpu.VMEM((micro * 2 * PIX, C), BF),
            pltpu.VMEM((micro * 2 * PIX, TAPS * 128), BF),
        ],
        flops=10**9, nbytes=2 * 10**6,
    )(cores, mine, other, hot)
    pieces = lax.all_to_all(part.reshape(blocks), ("dp", "py"), 0, 0, tiled=True)
    total = call(
        functools.partial(sum_kernel, rows // chips), jax.ShapeDtypeStruct((rows, 128), BF), [VMEM], nbytes=10**6,
    )(pieces.reshape((rows, 128)))
    full = lax.all_to_all(total.reshape(blocks), ("dp", "py"), 0, 0, tiled=True).reshape((rows, 128))
    swapped = lax.ppermute(full, "core", shift(2, 1))
    out_shape = jax.ShapeDtypeStruct((rows, C), BF)
    sem = [pltpu.SemaphoreType.DMA]
    half_done = call(functools.partial(place_kernel, 0), out_shape, [SMEM, ANY], sem, nbytes=10**6, out_spec=ANY)(
        cores, full)
    summed = call(functools.partial(place_kernel, 1), out_shape, [SMEM, ANY, ANY], sem, nbytes=10**6, aliases={2: 0},
                  out_spec=ANY)(cores, swapped, half_done)
    return (gin[None, :, None], summed[None])


def solution(mesh):
    size = dict(mesh.shape)
    grid = (size["dp"], size["section"], size["patch"] // 2, 2)
    fine = Mesh(mesh.devices.reshape(grid), ("dp", "section", "py", "core"))
    patch = ("py", "core")
    in_specs = (
        P(None, "dp", patch, None),
        P(None, "dp", patch, None),
        P("section", None, None),
        P(None, patch),
    )
    out_specs = (P("section", None, "dp", patch, None), P("section", None, None))
    return jax.shard_map(step, mesh=fine, in_specs=in_specs, out_specs=out_specs, check_vma=False)
```

```python
import functools

import jax
import jax.numpy as jnp
from jax import lax
from jax.experimental import pallas as pl
from jax.experimental.pallas import tpu as pltpu
from jax.sharding import Mesh
from jax.sharding import PartitionSpec as P


HALO = 32
TAPS = 9
C = 256
PIX = 96
LEVELS = 4
REACH = 2 * LEVELS * HALO
TILE = 64
PAD = 32
WIN = PIX + 2 * REACH
ROWS = WIN + 2 * PAD
HALF = TAPS * C // 2
BF = jnp.bfloat16
F32 = jnp.float32
NT = (((1,), (1,)), ((), ()))

FWD_ROWS = ((32, 576), (64, 544), (96, 512), (128, 480))
FWD_TILES = ((0, 9), (1, 9), (1, 8), (2, 8))
PRE_ROWS = ((224, 384), (192, 416), (160, 448), (128, 480))
BWD_ROWS = ((256, 352), (224, 384), (192, 416), (160, 448))
BWD_TILES = ((4, 6), (3, 6), (3, 7), (2, 7))
EDGE = 2 * HALO
OFF = 16
OWN = REACH
HROWS, PROWS, GROWS = PIX, PIX + HALO, PIX
MSG = HROWS + PROWS + GROWS


def expand(gat, t, src, hot):
    rows = jnp.dot(hot, src, preferred_element_type=F32).astype(BF)
    dst = pl.ds(pl.multiple_of(t * TILE, TILE), TILE)
    gat[dst, :C] = src[PAD:PAD + TILE]
    for k in range(1, TAPS):
        gat[dst, k * C:(k + 1) * C] = rows[(k - 1) * TILE:k * TILE]


def expand_all(gat, first, last, src_ref, hot_ref, group):
    def one(t):
        expand(gat, t, src_ref[pl.ds(pl.multiple_of(t * TILE, TILE), 2 * TILE), :], hot_ref[t])

    def some(i, carry):
        for j in range(group):
            one(first + i * group + j)
        return carry

    whole = (last - first) // group
    if whole:
        lax.fori_loop(0, whole, some, 0)
    for t in range(first + whole * group, last):
        one(t)


def pack_kernel(npix, ids_ref, maps, upstream, neighbours, own, to2a, to2b, to3a, to3b, off_buf):
    start, top = maps[0, 0], upstream[0, 0]
    place = ids_ref[2] * PIX + lax.broadcasted_iota(jnp.int32, (TAPS, PIX), 1)
    offsets = neighbours[...] - place + HALO
    offsets = jnp.where(offsets < 0, offsets + npix, offsets)
    offsets = jnp.where(offsets >= npix, offsets - npix, offsets) - HALO
    off_buf[...] = jnp.zeros_like(off_buf)
    off_buf[:TAPS, :PIX] = offsets.astype(F32)
    tail = off_buf[...].astype(BF)
    for ref, rows in ((own, (start, top)), (to2a, (start, top[PIX - HALO:])), (to2b, (start, top[:HALO])),
                      (to3a, (start[PIX - EDGE:],)), (to3b, (start[:EDGE],))):
        at = 0
        for value in (*rows, tail):
            ref[at:at + value.shape[0], :] = value
            at += value.shape[0]


def pack_call(ids, maps, upstream, neighbours):
    npix = PIX * lax.axis_size("py") * lax.axis_size("core")
    mine = pl.BlockSpec((1, 1, PIX, C), lambda i, ids: (ids[1], 0, 0, 0))
    rows = [2 * PIX + OFF, PIX + HALO + OFF, PIX + HALO + OFF, EDGE + OFF, EDGE + OFF]
    return pl.pallas_call(
        functools.partial(pack_kernel, npix),
        grid_spec=pltpu.PrefetchScalarGridSpec(
            num_scalar_prefetch=1,
            grid=(1,),
            in_specs=[mine, mine, pl.BlockSpec((TAPS, PIX), lambda i, ids: (0, 0))],
            out_specs=[pl.BlockSpec((n, C), lambda i, ids: (0, 0)) for n in rows],
            scratch_shapes=[pltpu.VMEM((OFF, C), F32)],
        ),
        out_shape=[jax.ShapeDtypeStruct((n, C), BF) for n in rows],
        interpret=INTERPRET,
        cost_estimate=pl.CostEstimate(flops=0, bytes_accessed=10**6, transcendentals=0),
    )(ids, maps, upstream, neighbours)


def prep_kernel(ids_ref, m3a, m2a, m1a, own, m1b, m2b, m3b, w_own, near_mine,
                h_ref, g_ref, s_ref, st_ref, gat_ref, pair_ref, w_ref, off_buf, sems):
    core, section = ids_ref[0], ids_ref[1]
    left, right = lax.rem(section + 3, LEVELS), lax.rem(section + 1, LEVELS)
    copies = []
    for n, (src, level) in enumerate((
        (w_own, section),
        (near_mine, jnp.where(core == 0, left, right)),
    )):
        copies.append(pltpu.make_async_copy(src, w_ref.at[level], sems.at[n]))
        copies[-1].start()
    h_ref[:PAD, :] = jnp.zeros((PAD, C), BF)
    h_ref[ROWS - PAD:, :] = jnp.zeros((PAD, C), BF)
    g_ref[...] = jnp.zeros_like(g_ref)
    off_buf[:PAD, :] = jnp.zeros((PAD, 128), F32)
    off_buf[ROWS - PAD:, :] = jnp.zeros((PAD, 128), F32)
    at = PAD
    shapes = ((EDGE, PIX - EDGE, 0, 0), (PIX, 0, HALO, PIX - HALO), (PIX, 0, PIX, 0), (PIX, 0, PIX, 0),
              (PIX, 0, PIX, 0), (PIX, 0, HALO, 0), (EDGE, 0, 0, 0))
    for piece, (n, first, n_top, first_top) in zip((m3a, m2a, m1a, own, m1b, m2b, m3b), shapes):
        h_ref[at:at + n, :] = piece[:n, :]
        if n_top:
            place = at + first_top
            g_ref[place:place + n_top, :] = piece[n:n + n_top, :]
        off_t = jnp.transpose(piece[n + n_top:, :128].astype(F32))
        off_buf[at:at + n, :OFF] = off_t[first:first + n]
        at += n

    rel = (lax.broadcasted_iota(jnp.int32, (TILE, 128), 1)
           - lax.broadcasted_iota(jnp.int32, (TILE, 128), 0) - HALO).astype(F32)

    def build_s(t, carry):
        d = off_buf[pl.ds(pl.multiple_of(t * TILE + PAD, PAD), TILE), :]
        for k in range(1, TAPS):
            hit = rel == d[:, k:k + 1]
            s_ref[t, (k - 1) * TILE:k * TILE, :] = jnp.where(hit, 1.0, 0.0).astype(BF)
        return carry

    lax.fori_loop(0, FWD_TILES[0][1], build_s, 0)

    def build_st(t, carry):
        d = jnp.transpose(off_buf[pl.ds(pl.multiple_of(t * TILE, TILE), 128), :])
        for k in range(1, TAPS):
            hit = -rel == d[k:k + 1, :]
            st_ref[t, (k - 1) * TILE:k * TILE, :] = jnp.where(hit, 1.0, 0.0).astype(BF)
        return carry

    lax.fori_loop(BWD_TILES[3][0], BWD_TILES[3][1], build_st, 0)
    expand_all(gat_ref, *FWD_TILES[0], h_ref, s_ref, 3)

    start = pl.multiple_of(PAD + OWN - HALO - PIX * core, HALO)
    offt = jnp.transpose(off_buf[pl.ds(start, 2 * PROWS), :])
    apart = (lax.broadcasted_iota(jnp.int32, (2 * PIX, 2 * PROWS), 0)
             - lax.broadcasted_iota(jnp.int32, (2 * PIX, 2 * PROWS), 1) + HALO).astype(F32)
    for k in range(1, TAPS):
        pair_ref[k - 1] = jnp.where(apart == offt[k:k + 1, :], 1.0, 0.0).astype(BF)
    for copy in copies:
        copy.wait()


def stack_kernel(ids_ref, h0, g_top, s_buf, st_buf, gat0, w_in, near_other, far_mine, far_other,
                 out_ref, w_buf, h_buf, gat, der, pre_buf, g_buf, sems):
    core, section = ids_ref[0], ids_ref[1]
    del w_in
    far = w_buf.at[lax.rem(section + 2, LEVELS)]
    copies = []
    for n, (src, dst) in enumerate((
        (near_other, w_buf.at[lax.rem(section + 1 + 2 * core, LEVELS)]),
        (far_mine, far.at[pl.ds(pl.multiple_of(core * HALF, HALF), HALF), :]),
        (far_other, far.at[pl.ds(pl.multiple_of((1 - core) * HALF, HALF), HALF), :]),
    )):
        copies.append(pltpu.make_async_copy(src, dst, sems.at[n]))
        copies[-1].start()
    h_buf[...] = jnp.zeros_like(h_buf)
    pre_buf[...] = jnp.zeros_like(pre_buf)
    g_buf[...] = g_top[...]
    for copy in copies:
        copy.wait()

    for level in range(LEVELS):
        first, last = FWD_TILES[level]

        src = h0 if level == 0 else h_buf.at[level - 1]
        rows = gat0 if level == 0 else gat
        if level:
            expand_all(gat, first, last, src, s_buf, 3)
        lo, hi = FWD_ROWS[level]
        act = jnp.dot(rows[lo:hi, :], w_buf[level], preferred_element_type=F32)
        squash = jnp.tanh(act)
        der[level, lo:hi, :] = 1.0 - squash * squash
        if level + 1 < LEVELS:
            h_buf[level, PAD + lo:PAD + hi, :] = (src[PAD + lo:PAD + hi, :].astype(F32) + squash).astype(BF)
        out_ref[level, :HROWS, :] = src[PAD + OWN:PAD + OWN + PIX, :]

    for level in range(LEVELS - 1, -1, -1):
        lo, hi = PRE_ROWS[level]
        pre_buf[PAD + lo:PAD + hi, :] = (
            g_buf[PAD + lo:PAD + hi, :].astype(F32) * der[level, lo:hi, :]).astype(BF)
        first, last = BWD_TILES[level]

        expand_all(gat, first, last, pre_buf, st_buf, 3)
        lo, hi = BWD_ROWS[level]
        total = g_buf[PAD + lo:PAD + hi, :].astype(F32)
        for k in range(TAPS):
            total = total + lax.dot_general(gat[lo:hi, k * C:(k + 1) * C],
                                            w_buf[level, k * C:(k + 1) * C, :], NT,
                                            preferred_element_type=F32)
        g_buf[PAD + lo:PAD + hi, :] = total.astype(BF)
        start = pl.multiple_of(PAD + OWN - HALO + HALO * core, HALO)
        out_ref[level, HROWS:HROWS + PROWS, :] = pre_buf[pl.ds(start, PROWS), :]
        out_ref[level, HROWS + PROWS:, :] = g_buf[PAD + OWN:PAD + OWN + PIX, :]


def grad_kernel(core_ref, mine, other, hot, out_ref, gin_ref, p_buf, h_buf, t_buf):
    core = core_ref[0]
    micro = mine.shape[0]
    pair = 2 * PIX
    gin_ref[...] = mine[:, HROWS + PROWS:, :]
    for c in range(2):
        @pl.when(core == c)
        def _(c=c):
            both = (mine, other) if c == 0 else (other, mine)
            for m in range(micro):
                for n, ref in enumerate(both):
                    p_buf[n * PROWS:(n + 1) * PROWS, m * 128:(m + 1) * 128] = (
                        ref[m, HROWS:HROWS + PROWS, c * 128:(c + 1) * 128])
                    h_buf[m * pair + n * PIX:m * pair + (n + 1) * PIX, :] = ref[m, :HROWS, :]
    h_t = jnp.transpose(h_buf[...].astype(F32)).astype(BF)
    pre = p_buf[...]
    for k in range(TAPS):
        if k == 0:
            spread = pre[HALO:HALO + pair]
        else:
            spread = jnp.dot(hot[k - 1], pre, preferred_element_type=F32).astype(BF)
        for m in range(micro):
            t_buf[m * pair:(m + 1) * pair, k * 128:(k + 1) * 128] = spread[:, m * 128:(m + 1) * 128]
        if k % 2 or k == TAPS - 1:
            low = k - k % 2 if k < TAPS - 1 else k
            block = jnp.dot(h_t, t_buf[:, low * 128:(k + 1) * 128], preferred_element_type=F32).astype(BF)
            for j in range(low, k + 1):
                out_ref[j * C:(j + 1) * C, :] = block[:, (j - low) * 128:(j - low + 1) * 128]


def sum_kernel(size, x_ref, out_ref):
    pairs = x_ref.shape[0] // (2 * size)
    total = x_ref[:2 * size, :].astype(F32)
    for n in range(1, pairs):
        total = total + x_ref[2 * size * n:2 * size * (n + 1), :].astype(F32)
    total = total[:size] + total[size:]
    total = jnp.concatenate([total, total]).astype(BF)
    for n in range(pairs):
        out_ref[2 * size * n:2 * size * (n + 1), :] = total


def place_kernel(side, core_ref, half, *refs):
    out_ref, sem = refs[-2:]
    column = pl.multiple_of(jnp.abs(core_ref[0] - side) * 128, 128)
    copy = pltpu.make_async_copy(half, out_ref.at[:, pl.ds(column, 128)], sem)
    copy.start()
    copy.wait()


VMEM = pl.BlockSpec(memory_space=pltpu.VMEM)
SMEM = pl.BlockSpec(memory_space=pltpu.SMEM)
ANY = pl.BlockSpec(memory_space=pl.ANY)
INTERPRET = False


def call(kernel, out_shape, in_specs, scratch=(), flops=0, nbytes=0, aliases=None, out_spec=None):
    many = isinstance(out_shape, (tuple, list))
    return pl.pallas_call(
        kernel,
        out_shape=out_shape,
        in_specs=in_specs,
        out_specs=[VMEM] * len(out_shape) if many else out_spec or VMEM,
        scratch_shapes=list(scratch),
        interpret=INTERPRET,
        input_output_aliases=aliases or {},
        cost_estimate=pl.CostEstimate(flops=flops, bytes_accessed=nbytes, transcendentals=0),
        compiler_params=pltpu.CompilerParams(vmem_limit_bytes=28 << 20),
    )


def prep_call(*operands):
    tiles, hot = FWD_TILES[0][1], (TAPS - 1) * TILE
    return call(
        prep_kernel,
        [
            jax.ShapeDtypeStruct((ROWS, C), BF),
            jax.ShapeDtypeStruct((ROWS, C), BF),
            jax.ShapeDtypeStruct((tiles, hot, 2 * TILE), BF),
            jax.ShapeDtypeStruct((BWD_TILES[3][1], hot, 2 * TILE), BF),
            jax.ShapeDtypeStruct((tiles * TILE, TAPS * C), BF),
            jax.ShapeDtypeStruct((TAPS - 1, 2 * PIX, 2 * PROWS), BF),
            jax.ShapeDtypeStruct((LEVELS, TAPS * C, C), BF),
        ],
        [SMEM] + [VMEM] * 7 + [ANY] * 2,
        [pltpu.VMEM((ROWS, 128), F32), pltpu.SemaphoreType.DMA((2,))],
        flops=10**9, nbytes=12 * 10**6,
    )(*operands)


def stack_call(*operands):
    tiles = FWD_TILES[0][1]
    return call(
        stack_kernel,
        [jax.ShapeDtypeStruct((LEVELS, MSG, C), BF), jax.ShapeDtypeStruct((LEVELS, TAPS * C, C), BF)],
        [SMEM] + [VMEM] * 6 + [ANY] * 3,
        [
            pltpu.VMEM((LEVELS - 1, ROWS, C), BF),
            pltpu.VMEM((tiles * TILE, TAPS * C), BF),
            pltpu.VMEM((LEVELS, tiles * TILE, C), F32),
            pltpu.VMEM((ROWS, C), BF),
            pltpu.VMEM((ROWS, C), BF),
            pltpu.SemaphoreType.DMA((3,)),
        ],
        flops=5 * 10**9, nbytes=10 * 10**6, aliases={6: 1},
    )(*operands)


def shift(axis_size, by):
    return [(i, (i + by) % axis_size) for i in range(axis_size)]


def step(maps, upstream, weights, neighbours):
    micro = maps.shape[0]
    section = lax.axis_index("section")
    core = lax.axis_index("core")
    patches = lax.axis_size("py") * lax.axis_size("core")
    patch = lax.axis_index("py") * lax.axis_size("core") + core
    cores = jnp.stack([core, section, patch]).astype(jnp.int32)

    sections = lax.axis_size("section")
    ways = [(2 * i + c, 2 * ((i + (1, -1)[c]) % sections) + c) for i in range(sections) for c in range(2)]
    near = lax.ppermute(weights[0], ("section", "core"), ways)
    half = lax.dynamic_slice_in_dim(near, core * HALF, HALF)
    far = lax.ppermute(half, ("section", "core"), ways)
    near_other = lax.ppermute(near, "core", shift(2, 1))
    far_other = lax.ppermute(far, "core", shift(2, 1))

    own, to2a, to2b, to3a, to3b = pack_call(cores, maps, upstream, neighbours)
    send = functools.partial(lax.ppermute, axis_name=("py", "core"))
    sends = []
    for block, by in ((to2b, -2), (own, -1), (own, 1), (to2a, 2), (to3b, -3), (to3a, 3)):
        sends.append(send(block, perm=shift(patches, by)))
    m2b, m1b, m1a, m2a, m3b, m3a = sends
    h0, g_top, s_hot, st_hot, gat0, hot, w_all = prep_call(
        cores, m3a, m2a, m1a, own, m1b, m2b, m3b, weights[0], near)
    out, _ = stack_call(cores, h0, g_top, s_hot, st_hot, gat0, w_all, near_other, far, far_other)

    mine = lax.all_to_all(out, "section", 0, 0, tiled=True)
    other = lax.ppermute(mine[:, :HROWS + PROWS], "core", shift(2, 1))
    chips = lax.axis_size("dp") * lax.axis_size("py")
    rows = TAPS * C
    blocks = (chips, rows // chips // 4, 4, 128)
    part, gin = call(
        grad_kernel,
        [jax.ShapeDtypeStruct((rows, 128), BF), jax.ShapeDtypeStruct((micro, PIX, C), BF)],
        [SMEM] + [VMEM] * 3,
        [
            pltpu.VMEM((2 * PROWS, micro * 128), BF),
            pltpu.VMEM((micro * 2 * PIX, C), BF),
            pltpu.VMEM((micro * 2 * PIX, TAPS * 128), BF),
        ],
        flops=10**9, nbytes=2 * 10**6,
    )(cores, mine, other, hot)
    pieces = lax.all_to_all(part.reshape(blocks), ("dp", "py"), 0, 0, tiled=True)
    total = call(
        functools.partial(sum_kernel, rows // chips), jax.ShapeDtypeStruct((rows, 128), BF), [VMEM], nbytes=10**6,
    )(pieces.reshape((rows, 128)))
    full = lax.all_to_all(total.reshape(blocks), ("dp", "py"), 0, 0, tiled=True).reshape((rows, 128))
    swapped = lax.ppermute(full, "core", shift(2, 1))
    out_shape = jax.ShapeDtypeStruct((rows, C), BF)
    sem = [pltpu.SemaphoreType.DMA]
    half_done = call(functools.partial(place_kernel, 0), out_shape, [SMEM, ANY], sem, nbytes=10**6, out_spec=ANY)(
        cores, full)
    summed = call(functools.partial(place_kernel, 1), out_shape, [SMEM, ANY, ANY], sem, nbytes=10**6, aliases={2: 0},
                  out_spec=ANY)(cores, swapped, half_done)
    return (gin[None, :, None], summed[None])


def solution(mesh):
    size = dict(mesh.shape)
    grid = (size["dp"], size["section"], size["patch"] // 2, 2)
    fine = Mesh(mesh.devices.reshape(grid), ("dp", "section", "py", "core"))
    patch = ("py", "core")
    in_specs = (
        P(None, "dp", patch, None),
        P(None, "dp", patch, None),
        P("section", None, None),
        P(None, patch),
    )
    out_specs = (P("section", None, "dp", patch, None), P("section", None, None))
    return jax.shard_map(step, mesh=fine, in_specs=in_specs, out_specs=out_specs, check_vma=False)
```
